256 devices in a mesh: sector: 32 (over z, y), mpo: 8 (over x, core).
Axes of the slice: x: 4, y: 4, z: 8, core: 2. Of those that a mesh axis runs over, the one named last changes fastest.
Arguments:
- guess: float32 [512, 128, 128], P('sector'), may hold values from -64 to 64
- diag_shift: float32 [512, 128, 128], P('sector'), may hold values from 0 to 6
- block_rows: int32 [512], P('sector'), may hold values from 64 to 128
- block_cols: int32 [512], P('sector'), may hold values from 64 to 128
- left_env: bfloat16 [64, 512, 128, 128], P('mpo', 'sector'), may hold values from -2 to 2
- right_env: bfloat16 [64, 512, 128, 128], P('mpo', 'sector'), may hold values from -2 to 2
- edge_input: int32 [1024], P('sector'), may hold values from 0 to 15
- edge_left: int32 [1024], P('sector'), may hold values from 0 to 15
- edge_right: int32 [1024], P('sector'), may hold values from 0 to 15
- edge_owner: int32 [1024, 1], P('sector'), may hold values from 0 to 31, as said below
- edge_slot: int32 [1024], P('sector'), may hold values from 0 to 15, as said below
Outputs:
- images: float32 [3, 512, 128, 128], P(None, 'sector', 'mpo')
- next_basis: float32 [512, 128, 128], P('sector', 'mpo')
- ritz: float32 [3], replicated
The draws below stay inside these ranges and needn't reach their ends.
Inputs may be any that keep to these rules, and one draw needn't show every extreme that they name: `edge_owner`: among the 32 couplings of one index of sector, at most 2 name the same owner, and some owner is named by exactly 2. No coupling names the index of sector that holds it. `edge_slot`: couplings come in mirrored pairs: for every coupling e there is a coupling f with in_f = out_e and out_f = in_e.
All inputs are finite; a program needn't handle non-finite values.
Results may differ from the reference program's by a relative error of at most 0.025.
Values may be sent and summed in bfloat16 or wider, within the bound.
No kernel may reach another device: no remote copies, remote signals or barrier semaphores. Data moves between devices by JAX's collectives and lax.ppermute only.
A program may use at most 64 MiB of HBM per device.

```python
import math
import jax
import jax.numpy as jnp
from jax import lax

P_SIZE = 128
W = 64
SLOT = 16
E_DEV = 32
LB = 16
APPLIES = 3
CAP = 2
BLOCKS = 512
EDGES = 1024
ENVS = 512
N_SECTOR = 32
N_MPO = 8


def pair_tables(key):
    base_key = jax.random.fold_in(key, 7001)
    key_rounds, key_reorder, key_slots = jax.random.split(base_key, 3)
    rounds = N_SECTOR - 1
    shuffled = jax.random.permutation(key_rounds, rounds).astype(jnp.int32)
    position = jnp.arange(E_DEV, dtype=jnp.int32)
    picked_index = jnp.where(position < CAP, 0, 1 + (position - CAP) % (N_SECTOR - 2)).astype(jnp.int32)
    round_list = shuffled[picked_index]
    reorder = jax.random.permutation(key_reorder, E_DEV).astype(jnp.int32)
    round_list = round_list[reorder]
    device = jnp.arange(N_SECTOR, dtype=jnp.int32)[:, None]
    chosen = round_list[None, :]
    opposite = (chosen - device) % rounds
    partner = jnp.where(device == N_SECTOR - 1, chosen * (N_SECTOR // 2) % rounds, jnp.where(opposite == device, N_SECTOR - 1, opposite)).astype(jnp.int32)
    in_slots = jax.random.randint(key_slots, (N_SECTOR, E_DEV), 0, SLOT, dtype=jnp.int32)
    columns = jnp.broadcast_to(position[None, :], (N_SECTOR, E_DEV))
    partner_slots = in_slots[partner, columns]
    return (in_slots, partner, partner_slots)


def draw_edge_input(key, part):
    in_slots, partner, partner_slots = pair_tables(key)
    return in_slots.reshape(EDGES).astype(jnp.int32)


def draw_edge_owner(key, part):
    in_slots, partner, partner_slots = pair_tables(key)
    return partner.reshape(EDGES, 1).astype(jnp.int32)


def draw_edge_slot(key, part):
    in_slots, partner, partner_slots = pair_tables(key)
    return partner_slots.reshape(EDGES).astype(jnp.int32)


def draw_guess(key, part):
    base_key = jax.random.fold_in(key, 911)
    key_rows, key_cols, key_blocks, key_common, key_own = jax.random.split(base_key, 5)
    row_scale = jnp.exp(jax.random.uniform(key_rows, (P_SIZE,), jnp.float32, 0.0, 0.5 * math.log(10.0)))
    col_scale = jnp.exp(jax.random.uniform(key_cols, (P_SIZE,), jnp.float32, 0.0, 0.5 * math.log(10.0)))
    rising = 1.0 + 2.0 * jnp.arange(BLOCKS, dtype=jnp.float32) / (BLOCKS - 1)
    block_scale = jnp.exp(jax.random.uniform(key_blocks, (BLOCKS,), jnp.float32, 0.0, math.log(10.0)))
    common = jnp.clip(jax.random.normal(key_common, (P_SIZE, P_SIZE), jnp.float32), -4.0, 4.0)
    own_part = 0.6 * jnp.clip(jax.random.normal(key_own, (BLOCKS, P_SIZE, P_SIZE), jnp.float32), -4.0, 4.0)
    field = row_scale[:, None] * col_scale[None, :] * (common[None, :, :] + own_part)
    return ((rising * block_scale)[:, None, None] * field / 48.0).astype(jnp.float32)


def env_noise(key, shape):
    return jnp.clip(jax.random.normal(key, shape, jnp.float32), -4.0, 4.0)


def draw_left_env(key, part):
    base_key = jax.random.fold_in(key, 1301)
    key_match, key_amp, key_noise = jax.random.split(base_key, 3)
    group_size = W // N_MPO
    band_size = P_SIZE // N_MPO
    matching = jax.random.permutation(key_match, N_MPO).astype(jnp.int32)
    term_group = jnp.arange(W, dtype=jnp.int32) // group_size
    row_band = jnp.arange(P_SIZE, dtype=jnp.int32) // band_size
    strong = (matching[term_group][:, None] == row_band[None, :]).astype(jnp.float32)
    amplitude = jax.random.uniform(key_amp, (W, ENVS, P_SIZE), jnp.float32, 0.5, 1.5) * (2.0 / group_size) * strong[:, None, :]
    noise = env_noise(key_noise, (W, ENVS, P_SIZE, P_SIZE)) * (0.6 / math.sqrt(W * P_SIZE))
    on_diagonal = jnp.arange(P_SIZE, dtype=jnp.int32)[:, None] == jnp.arange(P_SIZE, dtype=jnp.int32)[None, :]
    values = noise + jnp.where(on_diagonal, amplitude[:, :, :, None], 0.0)
    return values.astype(jnp.bfloat16)


def draw_right_env(key, part):
    base_key = jax.random.fold_in(key, 1709)
    key_amp, key_noise = jax.random.split(base_key, 2)
    amplitude = jax.random.uniform(key_amp, (W, ENVS, P_SIZE), jnp.float32, 0.5, 1.5)
    noise = env_noise(key_noise, (W, ENVS, P_SIZE, P_SIZE)) * (0.3 / math.sqrt(P_SIZE))
    on_diagonal = jnp.arange(P_SIZE, dtype=jnp.int32)[:, None] == jnp.arange(P_SIZE, dtype=jnp.int32)[None, :]
    values = noise + jnp.where(on_diagonal, amplitude[:, :, :, None], 0.0)
    return values.astype(jnp.bfloat16)


def set_ends(entries, key, low, largest):
    longest = entries.shape.index(max(entries.shape))
    spots = []
    for shift in (0, 1):
        where = [jax.random.randint(jax.random.fold_in(key, axis), (), 0, length) for axis, length in enumerate(entries.shape)]
        where[longest] = (where[longest] + shift) % entries.shape[longest]
        spots.append(tuple(where))
    return entries.at[spots[0]].set(low).at[spots[1]].set(largest)


def shard_levels(stream_key, shape, shards, least, largest):
    loudness = 1.0
    for dim, shards_of in shards:
        heights = jax.random.uniform(jax.random.fold_in(jax.random.fold_in(stream_key, 6), dim), (shards_of,), jnp.float32, least / len(shards), largest / len(shards))
        loudness = loudness * jnp.repeat(jnp.exp(heights), shape[dim] // shards_of).reshape((-1,) + (1,) * (len(shape) - 1 - dim))
    return loudness


def setup_inputs(seed: int = 0) -> dict:
    splits = jax.random.split(jax.random.key(seed), 12)
    guess = draw_guess(jax.random.fold_in(splits[11], 71), 0)
    diag_shift = jnp.clip(6.0 * jax.random.uniform(splits[1], (BLOCKS, P_SIZE, P_SIZE), jnp.float32) ** shard_levels(splits[1], (BLOCKS, P_SIZE, P_SIZE), ((0, 32),), -0.2, 0.2), 0.0, 6.0)
    block_rows = set_ends(jax.random.randint(splits[2], (BLOCKS,), P_SIZE // 2, P_SIZE + 1), jax.random.fold_in(splits[2], 1), P_SIZE // 2, P_SIZE).astype(jnp.int32)
    block_cols = set_ends(jax.random.randint(splits[3], (BLOCKS,), P_SIZE // 2, P_SIZE + 1), jax.random.fold_in(splits[3], 1), P_SIZE // 2, P_SIZE).astype(jnp.int32)
    left_env = draw_left_env(jax.random.fold_in(splits[11], 71), 0)
    right_env = draw_right_env(jax.random.fold_in(splits[11], 71), 0)
    edge_input = draw_edge_input(jax.random.fold_in(splits[11], 71), 0)
    edge_left = set_ends(jax.random.randint(splits[7], (EDGES,), 0, LB), jax.random.fold_in(splits[7], 1), 0, LB - 1).astype(jnp.int32)
    edge_right = set_ends(jax.random.randint(splits[8], (EDGES,), 0, LB), jax.random.fold_in(splits[8], 1), 0, LB - 1).astype(jnp.int32)
    edge_owner = draw_edge_owner(jax.random.fold_in(splits[11], 71), 0)
    edge_slot = draw_edge_slot(jax.random.fold_in(splits[11], 71), 0)
    return {"guess": guess, "diag_shift": diag_shift, "block_rows": block_rows, "block_cols": block_cols, "left_env": left_env, "right_env": right_env, "edge_input": edge_input, "edge_left": edge_left, "edge_right": edge_right, "edge_owner": edge_owner, "edge_slot": edge_slot}


def coupling_terms(xin, left_env, right_env, in_global, left_global, right_global):
    group = W // N_MPO
    left_groups = left_env.reshape(N_MPO, group, ENVS, P_SIZE, P_SIZE)
    right_groups = right_env.reshape(N_MPO, group, ENVS, P_SIZE, P_SIZE)

    def one_block(indices):
        inputs, lefts, rights = indices
        picked = xin[inputs].astype(jnp.float32)

        def one_group(envs):
            left_group, right_group = envs

            def one_term(total, pair):
                left_term, right_term = pair
                half = jnp.einsum('eij,ejk->eik', picked, right_term[rights].astype(jnp.float32))
                half = half.astype(jnp.bfloat16).astype(jnp.float32)
                return (total + jnp.einsum('eij,ejk->eik', left_term[lefts].astype(jnp.float32), half), None)
            total, _ = lax.scan(one_term, jnp.zeros((E_DEV, P_SIZE, P_SIZE), jnp.float32), (left_group, right_group))
            return total.astype(jnp.bfloat16)
        parts = lax.map(one_group, (left_groups, right_groups))
        return lax.optimization_barrier(jnp.sum(parts.astype(jnp.float32), axis=0)).astype(jnp.bfloat16)
    blocks = lax.map(one_block, (in_global.reshape(N_SECTOR, E_DEV), left_global.reshape(N_SECTOR, E_DEV), right_global.reshape(N_SECTOR, E_DEV)))
    return blocks.reshape(EDGES, P_SIZE, P_SIZE)

def reference(guess, diag_shift, block_rows, block_cols, left_env, right_env, edge_input, edge_left, edge_right, edge_owner, edge_slot):
    rows_index = lax.broadcasted_iota(jnp.int32, (BLOCKS, P_SIZE, P_SIZE), 1)
    cols_index = lax.broadcasted_iota(jnp.int32, (BLOCKS, P_SIZE, P_SIZE), 2)
    mask = ((rows_index < block_rows[:, None, None]) & (cols_index < block_cols[:, None, None])).astype(jnp.float32)
    source = (jnp.arange(EDGES, dtype=jnp.int32) // E_DEV).astype(jnp.int32)
    in_global = (source * SLOT + edge_input).astype(jnp.int32)
    left_global = (source * LB + edge_left).astype(jnp.int32)
    right_global = (source * LB + edge_right).astype(jnp.int32)
    out_global = (edge_owner[:, 0] * SLOT + edge_slot).astype(jnp.int32)
    start = mask * guess
    basis = [start / jnp.sqrt(jnp.sum(start * start) + 1e-06)]
    image_list = []
    ritz_list = []
    for step in range(APPLIES):
        current = basis[-1]
        xin = current.astype(jnp.bfloat16)
        contrib = coupling_terms(xin, left_env, right_env, in_global, left_global, right_global)
        image = jax.ops.segment_sum(contrib.astype(jnp.float32), out_global, num_segments=BLOCKS) * mask
        image_list.append(image)
        theta = jnp.sum(current * image)
        ritz_list.append(theta)
        corr = mask * (image - theta * current) / jnp.maximum(jnp.abs(diag_shift - theta), 1.0)
        ortho = corr
        for vector in basis:
            ortho = ortho - jnp.sum(vector * corr) * vector
        basis.append(ortho / jnp.sqrt(jnp.sum(ortho * ortho) + 1e-06))
    return (jnp.stack(image_list), basis[-1], jnp.stack(ritz_list))
```

```python
import jax
import jax.numpy as jnp
from jax import lax
from jax.experimental import pallas as pl
from jax.experimental.pallas import tpu as pltpu
from jax.sharding import PartitionSpec as P

APPLIES = 3
CAP = 2
EXTRA = 8
ID_ROW = 4
UNROLL = 4
BF = jnp.bfloat16
F32 = jnp.float32
VMEM = pl.BlockSpec(memory_space=pltpu.VMEM)
SMEM = pl.BlockSpec(memory_space=pltpu.SMEM)
ROW_IN, ROW_LEFT, ROW_RIGHT, ROW_OWNER, ROW_SLOT, ROW_ROWS, ROW_COLS, ROW_POS = range(8)


def call(body, name, in_specs, out_shape, scratch=(), mib=8):
    return pl.pallas_call(
        body,
        name=name,
        in_specs=in_specs,
        out_shape=out_shape,
        out_specs=jax.tree.map(lambda _: VMEM, out_shape),
        scratch_shapes=scratch,
        compiler_params=pltpu.CompilerParams(vmem_limit_bytes=mib << 20),
    )


def out(shape, dtype):
    return jax.ShapeDtypeStruct(shape, dtype)


def total(values):
    return jnp.sum(jnp.sum(values, axis=0, keepdims=True), axis=1, keepdims=True)


def fold(values):
    return jnp.sum(values.reshape(-1, 8, values.shape[-1]), axis=0)


def three_parts(value, row, height):
    high = value.astype(BF).astype(F32)
    middle = (value - high).astype(BF).astype(F32)
    low = value - high - middle
    lane = lax.broadcasted_iota(jnp.int32, (height, 128), 1)
    line = lax.broadcasted_iota(jnp.int32, (height, 128), 0)
    spread = jnp.where(lane == 0, high, jnp.where(lane == 1, middle, jnp.where(lane == 2, low, 0.0)))
    return jnp.where(line == row, spread, 0.0)


def mask_of(meta, block, shape, first_row):
    line = lax.broadcasted_iota(jnp.int32, shape, 0) + first_row
    lane = lax.broadcasted_iota(jnp.int32, shape, 1)
    return (line < meta[ROW_ROWS, block]) & (lane < meta[ROW_COLS, block])


def start_kernel(slots, size, share):
    def body(meta, guess, vector, xin, own, sums):
        acc = jnp.zeros((8, size), F32)
        first_row = pl.multiple_of(meta[ROW_POS, 0] * share, share)
        for b in range(slots):
            value = jnp.where(mask_of(meta, b, (size, size), 0), guess[b], 0.0)
            vector[b] = value
            xin[b] = value.astype(BF)
            acc = acc + fold(value * value)
            mine = guess[b, pl.ds(first_row, share)]
            own[b] = jnp.where(mask_of(meta, b, (share, size), first_row), mine, 0.0)
        sums[...] = three_parts(total(acc), 0, EXTRA)

    return call(
        body,
        "start",
        [SMEM, VMEM],
        (
            out((slots, size, size), F32),
            out((slots, size, size), BF),
            out((slots, share, size), F32),
            out((EXTRA, size), F32),
        ),
    )


def couple_kernel(edges, size, share, group, chips):
    def body(meta, xin, right, left, own, send, tmp):
        x = meta[ROW_POS, 1]
        c = meta[ROW_POS, 2]

        def one(e, u):
            i = meta[ROW_IN, e]
            le = meta[ROW_LEFT, e]
            re = meta[ROW_RIGHT, e]
            value = xin[i]
            acc = None
            for w in range(group):
                half = jnp.dot(value, right[w, re], preferred_element_type=F32).astype(BF)
                term = jnp.dot(left[w, le], half, preferred_element_type=F32)
                acc = term if acc is None else acc + term
            tmp[u] = acc.astype(BF)
            for k in range(chips):
                to = lax.rem(x + k, chips)
                mine = pl.multiple_of((2 * to + c) * share, share)
                other = pl.multiple_of((2 * to + 1 - c) * share, share)
                own[k, e] = tmp[u, pl.ds(mine, share)]
                send[k, e] = tmp[u, pl.ds(other, share)]

        def step(t, carry):
            for u in range(UNROLL):
                one(t * UNROLL + u, u)
            return carry

        lax.fori_loop(0, edges // UNROLL, step, 0)

    shape = out((chips, edges, share, size), BF)
    return call(
        body,
        "couple",
        [SMEM, VMEM, VMEM, VMEM],
        (shape, shape),
        [pltpu.VMEM((UNROLL, size, size), BF)],
    )


def pair_kernel(edges, size, share, chips):
    def body(own, received, *parts):
        for k in range(chips):
            parts[k][...] = (own[k].astype(F32) + received[k].astype(F32)).astype(BF)

    return call(
        body, "pair", [VMEM, VMEM], tuple(out((edges, share, size), BF) for _ in range(chips))
    )


def pack_kernel(edges, size, share, sectors, with_ids):
    height = CAP * share + EXTRA

    def body(meta, sums, first, second, third, fourth, message, seen):
        message[...] = jnp.zeros_like(message)
        line = lax.broadcasted_iota(jnp.int32, (EXTRA, size), 0)
        lane = lax.broadcasted_iota(jnp.int32, (EXTRA, size), 1)
        tail = sums[...]
        if with_ids:
            tail = jnp.where((line == ID_ROW) & (lane < CAP), -1.0, tail)
        for s in range(sectors):
            seen[s] = 0
            message[s, CAP * share :] = tail.astype(BF)
        for e in range(edges):
            owner = meta[ROW_OWNER, e]
            rank = seen[owner]
            seen[owner] = rank + 1
            value = first[e].astype(F32) + second[e].astype(F32)
            value = value + (third[e].astype(F32) + fourth[e].astype(F32))
            message[owner, pl.ds(pl.multiple_of(rank * share, share), share)] = value.astype(BF)
            if with_ids:
                slot = meta[ROW_SLOT, e].astype(F32)
                here = message[owner, CAP * share :].astype(F32)
                here = jnp.where((line == ID_ROW) & (lane == rank), slot, here)
                message[owner, CAP * share :] = here.astype(BF)

    return call(
        body,
        "pack",
        [SMEM] + [VMEM] * 5,
        out((sectors, height, size), BF),
        [pltpu.SMEM((sectors,), jnp.int32)],
    )


def image_kernel(k, slots, size, share, sectors):
    def body(meta, ids, arrived, vector, state, *refs):
        bases = refs[: k - 1]
        images = refs[k - 1 : 2 * k - 2]
        image, basis, message, new_state, acc = refs[2 * k - 2 :]
        sums = jnp.zeros((EXTRA, size), F32)
        acc[...] = jnp.zeros_like(acc)
        for s in range(sectors):
            sums = sums + arrived[s, CAP * share :].astype(F32)
            for c in range(CAP):
                slot = ids[s * CAP + c]
                acc[slot] = acc[slot] + arrived[s, c * share : (c + 1) * share].astype(F32)
        sums = jnp.sum(sums, axis=1, keepdims=True)
        total_of = [sums[j : j + 1] for j in range(k)]
        new_state[...] = state[...]

        def gram(i, j):
            row = 8 + 4 * max(i, j) + min(i, j)
            return state[row : row + 1, 0:1]

        def keep(row, value):
            new_state[row : row + 1] = jnp.broadcast_to(value, (1, size))

        project = total_of[: k - 1]
        length = total_of[k - 1]
        crossed = []
        for i in range(k - 1):
            mixed = jnp.zeros((1, 1), F32)
            for j in range(k - 1):
                mixed = mixed + gram(i, j) * project[j]
            crossed.append(mixed)
            length = length + project[i] * (mixed - 2.0 * project[i])
        length = jnp.maximum(length, 0.0)
        scale = 1.0 / jnp.sqrt(length + 1e-6)
        keep(4, scale)
        for j in range(k - 1):
            keep(5 + j, project[j])
            keep(8 + 4 * (k - 1) + j, scale * (project[j] - crossed[j]))
        keep(8 + 4 * (k - 1) + k - 1, length * scale * scale)
        first_row = meta[ROW_POS, 0] * share
        theta = jnp.zeros((8, size), F32)
        for b in range(slots):
            value = jnp.where(mask_of(meta, b, (share, size), first_row), acc[b], 0.0)
            direction = vector[b]
            for j in range(k - 1):
                value = value - project[j] * images[j][b]
                direction = direction - project[j] * bases[j][b]
            value = value * scale
            direction = direction * scale
            image[b] = value
            basis[b] = direction
            message[b] = value.astype(BF)
            theta = theta + fold(value * direction)
        message[slots] = three_parts(total(theta), 0, share).astype(BF)

    return call(
        body,
        "image",
        [SMEM, SMEM] + [VMEM] * (3 + 2 * (k - 1)),
        (
            out((slots, share, size), F32),
            out((slots, share, size), F32),
            out((slots + 1, share, size), BF),
            out((24, size), F32),
        ),
        [pltpu.VMEM((slots + 1, share, size), F32)],
    )


def spread_kernel(slots, size, sectors):
    def body(gathered, message):
        value = total(gathered[slots].astype(F32))
        message[...] = jnp.broadcast_to(value[None], (sectors, 1, size))

    return call(body, "spread", [VMEM], out((sectors, 1, size), F32))


def correct_kernel(k, slots, size, share, sectors, last):
    def body(meta, thetas, gathered, vector, shift, image, basis, state, *refs):
        bases = refs[: k - 1]
        if last:
            corrected, sums, new_state = refs[k - 1 :]
        else:
            whole_basis, whole, xin, corrected, sums, new_state = refs[k - 1 :]
        theta = jnp.sum(thetas[...].reshape(sectors, size), axis=0, keepdims=True)
        new_state[...] = state[...]
        new_state[k - 1 : k] = theta
        scale = state[4:5]
        project = [state[5 + j : 6 + j] for j in range(k - 1)]
        first_row = pl.multiple_of(meta[ROW_POS, 0] * share, share)

        def residual(mask, value, direction, moved):
            bottom = jnp.maximum(jnp.abs(moved - theta), 1.0)
            return jnp.where(mask, (value - theta * direction) / bottom, 0.0)

        def step(b, carry):
            direction = vector[b]
            for j in range(k - 1):
                direction = direction - project[j] * bases[j][b]
            direction = direction * scale
            value = residual(
                mask_of(meta, b, (size, size), 0),
                gathered[b].astype(F32),
                direction,
                shift[b],
            )
            if not last:
                whole_basis[b] = direction
                whole[b] = value
                xin[b] = value.astype(BF)
            corrected[b] = residual(
                mask_of(meta, b, (share, size), first_row),
                image[b],
                basis[b],
                shift[b, pl.ds(first_row, share)],
            )
            others = [bases[j][b] for j in range(k - 1)] + [direction, value]
            return tuple(a + fold(value * o) for a, o in zip(carry, others))

        carry = lax.fori_loop(
            0, slots, step, tuple(jnp.zeros((8, size), F32) for _ in range(k + 1)), unroll=2
        )
        if last:
            line = lax.broadcasted_iota(jnp.int32, (EXTRA, size), 0)
            tail = jnp.zeros((EXTRA, size), F32)
            for j in range(k + 1):
                tail = jnp.where(line == j, total(carry[j]), tail)
            sums[...] = jnp.broadcast_to(tail[None], (sectors, EXTRA, size))
        else:
            tail = jnp.zeros((EXTRA, size), F32)
            for j in range(k + 1):
                tail = tail + three_parts(total(carry[j]), j, EXTRA)
            sums[...] = tail

    blocks = out((slots, size, size), F32)
    shapes = [out((slots, share, size), F32), out((EXTRA, size), F32), out((24, size), F32)]
    if last:
        shapes[1] = out((sectors, EXTRA, size), F32)
    else:
        shapes = [blocks, blocks, out((slots, size, size), BF)] + shapes
    return call(body, "correct", [SMEM] + [VMEM] * (6 + k), tuple(shapes))


def finish_kernel(slots, size, share, sectors):
    k = APPLIES

    def body(sums, vector, state, *refs):
        bases = refs[:k]
        images = refs[k : 2 * k]
        stacked, final, ritz = refs[2 * k :]
        added = jnp.sum(sums[...], axis=0)
        project = [added[j : j + 1] for j in range(k)]
        length = added[k : k + 1]
        for i in range(k):
            mixed = jnp.zeros((1, size), F32)
            for j in range(k):
                row = 8 + 4 * max(i, j) + min(i, j)
                mixed = mixed + state[row : row + 1] * project[j]
            length = length + project[i] * (mixed - 2.0 * project[i])
        scale = 1.0 / jnp.sqrt(jnp.maximum(length, 0.0) + 1e-6)
        for b in range(slots):
            value = vector[b]
            for j in range(k):
                value = value - project[j] * bases[j][b]
            final[b] = value * scale
            for j in range(k):
                stacked[j, b] = images[j][b]
        ritz[...] = state[0:8]

    return call(
        body,
        "finish",
        [VMEM] * (3 + 2 * k),
        (
            out((k, slots, share, size), F32),
            out((slots, share, size), F32),
            out((8, size), F32),
        ),
    )


def per_device(
    guess,
    diag_shift,
    block_rows,
    block_cols,
    left_env,
    right_env,
    edge_input,
    edge_left,
    edge_right,
    edge_owner,
    edge_slot,
):
    slots, size, _ = guess.shape
    sectors = lax.axis_size("sector")
    terms = lax.axis_size("mpo")
    edges = edge_input.shape[0]
    group = left_env.shape[0]
    share = size // terms
    chips = terms // 2
    place = lax.axis_index("mpo")
    core_swap = [(i, i ^ 1) for i in range(terms)]
    pos = jnp.stack([place, place // 2, place % 2]).astype(jnp.int32)

    def wide(row):
        return jnp.pad(row, (0, edges - row.shape[0]))

    meta = jnp.stack(
        [
            edge_input,
            edge_left,
            edge_right,
            edge_owner[:, 0],
            edge_slot,
            wide(block_rows),
            wide(block_cols),
            wide(pos),
        ]
    )

    def over_sector(values):
        return lax.all_to_all(values, "sector", 0, 0, tiled=True)

    def chip_shift(values, k):
        pairs = [(i, (i + 2 * k) % terms) for i in range(terms)]
        return lax.ppermute(values, "mpo", pairs)

    vector, xin, mine, sums = start_kernel(slots, size, share)(meta, guess)
    state = jnp.zeros((24, size), F32)
    bases, images, whole_bases = [], [], []
    ids = None
    for k in range(1, APPLIES + 1):
        own, send = couple_kernel(edges, size, share, group, chips)(
            meta, xin, right_env, left_env
        )
        received = lax.ppermute(send, "mpo", core_swap)
        parts = pair_kernel(edges, size, share, chips)(own, received)
        shifted = [parts[0]] + [chip_shift(parts[j], j) for j in range(1, chips)]
        message = pack_kernel(edges, size, share, sectors, k == 1)(meta, sums, *shifted)
        arrived = over_sector(message)
        if ids is None:
            ids = arrived[:, CAP * share + ID_ROW, :CAP].astype(jnp.int32).reshape(-1)
            ids = jnp.where(ids < 0, slots, ids)
        image, basis, outgoing, state = image_kernel(k, slots, size, share, sectors)(
            meta, ids, arrived, mine, state, *bases, *images
        )
        gathered = lax.all_gather(outgoing, "mpo", axis=1, tiled=True)
        thetas = over_sector(spread_kernel(slots, size, sectors)(gathered))
        last = k == APPLIES
        result = correct_kernel(k, slots, size, share, sectors, last)(
            meta, thetas, gathered, vector, diag_shift, image, basis, state, *whole_bases
        )
        if last:
            mine, sums, state = result
        else:
            whole_basis, vector, xin, mine, sums, state = result
            whole_bases.append(whole_basis)
        bases.append(basis)
        images.append(image)
    stacked, final, ritz = finish_kernel(slots, size, share, sectors)(
        over_sector(sums), mine, state, *bases, *images
    )
    return stacked, final, ritz[:APPLIES, 0]


def solution(mesh):
    return jax.shard_map(
        per_device,
        mesh=mesh,
        in_specs=(
            P("sector", None, None),
            P("sector", None, None),
            P("sector"),
            P("sector"),
            P("mpo", "sector", None, None),
            P("mpo", "sector", None, None),
            P("sector"),
            P("sector"),
            P("sector"),
            P("sector", None),
            P("sector"),
        ),
        out_specs=(P(None, "sector", "mpo", None), P("sector", "mpo", None), P()),
        check_vma=False,
    )
```

```python
import jax
import jax.numpy as jnp
from jax import lax
from jax.experimental import pallas as pl
from jax.experimental.pallas import tpu as pltpu
from jax.sharding import PartitionSpec as P

APPLIES = 3
CAP = 2
EXTRA = 8
ID_ROW = 4
UNROLL = 4
BF = jnp.bfloat16
F32 = jnp.float32
VMEM = pl.BlockSpec(memory_space=pltpu.VMEM)
SMEM = pl.BlockSpec(memory_space=pltpu.SMEM)
FAR = pl.BlockSpec(memory_space=pltpu.HBM)
ROW_IN, ROW_LEFT, ROW_RIGHT, ROW_OWNER, ROW_SLOT, ROW_SIZES, ROW_POS = range(7)
PIECES = 4


def call(body, name, in_specs, out_shape, scratch=(), mib=8, aliases={}, out_specs=None):
    return pl.pallas_call(
        body,
        name=name,
        in_specs=in_specs,
        out_shape=out_shape,
        out_specs=out_specs or jax.tree.map(lambda _: VMEM, out_shape),
        input_output_aliases=aliases,
        scratch_shapes=scratch,
        compiler_params=pltpu.CompilerParams(vmem_limit_bytes=mib << 20),
    )


def out(shape, dtype):
    return jax.ShapeDtypeStruct(shape, dtype)


def total(values):
    return jnp.sum(jnp.sum(values, axis=0, keepdims=True), axis=1, keepdims=True)


def fold(values):
    return jnp.sum(values.reshape(-1, 8, values.shape[-1]), axis=0)


def three_parts(value, row, height):
    high = value.astype(BF).astype(F32)
    middle = (value - high).astype(BF).astype(F32)
    low = value - high - middle
    lane = lax.broadcasted_iota(jnp.int32, (height, 128), 1)
    line = lax.broadcasted_iota(jnp.int32, (height, 128), 0)
    spread = jnp.where(lane == 0, high, jnp.where(lane == 1, middle, jnp.where(lane == 2, low, 0.0)))
    return jnp.where(line == row, spread, 0.0)


def mask_of(meta, block, slots, shape, first_row):
    line = lax.broadcasted_iota(jnp.int32, shape, 0) + first_row
    lane = lax.broadcasted_iota(jnp.int32, shape, 1)
    return (line < meta[ROW_SIZES, block]) & (lane < meta[ROW_SIZES, slots + block])


def start_kernel(slots, size, share, group):
    def body(meta, far_guess, right, left, *refs):
        vector, xin, own, sums, state, right_near, left_near, guess, sems, guess_sem = refs
        state[...] = jnp.zeros_like(state)
        first = pltpu.make_async_copy(far_guess, guess, guess_sem)
        first.start()
        copies = []
        for i, (far, near) in enumerate(((right, right_near), (left, left_near))):
            for p in range(PIECES):
                part = pl.ds(p * (group // PIECES), group // PIECES)
                copies.append(pltpu.make_async_copy(far.at[part], near.at[part], sems.at[i, p]))
        for copy in copies:
            copy.start()
        acc = jnp.zeros((8, size), F32)
        first_row = pl.multiple_of(meta[ROW_POS, 0] * share, share)
        first.wait()
        for b in range(slots):
            value = jnp.where(mask_of(meta, b, slots, (size, size), 0), guess[b], 0.0)
            vector[b] = value
            xin[b] = value.astype(BF)
            acc = acc + fold(value * value)
            mine = guess[b, pl.ds(first_row, share)]
            own[b] = jnp.where(mask_of(meta, b, slots, (share, size), first_row), mine, 0.0)
        sums[...] = three_parts(total(acc), 0, EXTRA)
        for copy in copies:
            copy.wait()

    near = pltpu.VMEM((group, slots, size, size), BF)
    return call(
        body,
        "start",
        [SMEM, FAR, FAR, FAR],
        (
            out((slots, size, size), F32),
            out((slots, size, size), BF),
            out((slots, share, size), F32),
            out((EXTRA, size), F32),
            out((24, size), F32),
            near,
            near,
        ),
        [
            pltpu.VMEM((slots, size, size), F32),
            pltpu.SemaphoreType.DMA((2, PIECES)),
            pltpu.SemaphoreType.DMA,
        ],
    )


def couple_kernel(edges, slots, size, share, group, chips):
    def body(meta, xin, right, left, own, send, *refs):
        tmp = refs[-1]
        x = meta[ROW_POS, 1]
        c = meta[ROW_POS, 2]

        def one(e, u):
            i = meta[ROW_IN, e]
            le = meta[ROW_LEFT, e]
            re = meta[ROW_RIGHT, e]
            value = xin[i]
            acc = None
            for w in range(group):
                half = jnp.dot(value, right[w, re], preferred_element_type=F32).astype(BF)
                term = jnp.dot(left[w, le], half, preferred_element_type=F32)
                acc = term if acc is None else acc + term
            tmp[u] = acc.astype(BF)
            for k in range(chips):
                to = lax.rem(x + k, chips)
                mine = pl.multiple_of((2 * to + c) * share, share)
                other = pl.multiple_of((2 * to + 1 - c) * share, share)
                own[k, e] = tmp[u, pl.ds(mine, share)]
                send[k, e] = tmp[u, pl.ds(other, share)]

        def step(t, carry):
            for u in range(UNROLL):
                one(t * UNROLL + u, u)
            return carry

        lax.fori_loop(0, edges // UNROLL, step, 0)

    shape = out((chips, edges, share, size), BF)
    near = pltpu.VMEM((group, slots, size, size), BF)
    return call(
        body,
        "couple",
        [SMEM, VMEM, VMEM, VMEM],
        (shape, shape, near, near),
        [pltpu.VMEM((UNROLL, size, size), BF)],
        aliases={2: 2, 3: 3},
    )


def pair_kernel(edges, size, share, chips):
    def body(own, received, *parts):
        for k in range(chips):
            parts[k][...] = (own[k].astype(F32) + received[k].astype(F32)).astype(BF)

    return call(
        body, "pair", [VMEM, VMEM], tuple(out((edges, share, size), BF) for _ in range(chips))
    )


def pack_kernel(edges, size, share, sectors):
    height = CAP * share + EXTRA

    def body(meta, sums, first, second, third, fourth, message, seen):
        message[...] = jnp.zeros_like(message)
        line = lax.broadcasted_iota(jnp.int32, (EXTRA, size), 0)
        lane = lax.broadcasted_iota(jnp.int32, (EXTRA, size), 1)
        tail = sums[...]
        tail = jnp.where((line == ID_ROW) & (lane < CAP), -1.0, tail)
        for s in range(sectors):
            seen[s] = 0
            message[s, CAP * share :] = tail.astype(BF)
        for e in range(edges):
            owner = meta[ROW_OWNER, e]
            rank = seen[owner]
            seen[owner] = rank + 1
            value = first[e].astype(F32) + second[e].astype(F32)
            value = value + (third[e].astype(F32) + fourth[e].astype(F32))
            message[owner, pl.ds(pl.multiple_of(rank * share, share), share)] = value.astype(BF)
            slot = meta[ROW_SLOT, e].astype(F32)
            here = message[owner, CAP * share :].astype(F32)
            here = jnp.where((line == ID_ROW) & (lane == rank), slot, here)
            message[owner, CAP * share :] = here.astype(BF)

    return call(
        body,
        "pack",
        [SMEM] + [VMEM] * 5,
        out((sectors, height, size), BF),
        [pltpu.SMEM((sectors,), jnp.int32)],
    )


def image_kernel(k, slots, size, share, sectors):
    def body(meta, arrived, vector, state, *refs):
        bases = refs[: k - 1]
        images = refs[k - 1 : 2 * k - 2]
        image, basis, message, new_state, acc, slot_lanes, ids = refs[2 * k - 2 :]
        line = lax.broadcasted_iota(jnp.int32, (EXTRA, size), 0)
        for s in range(sectors):
            tail = arrived[s, CAP * share :].astype(F32)
            slot = jnp.sum(jnp.where(line == ID_ROW, tail, 0.0), axis=0, keepdims=True)
            slot_lanes[s : s + 1] = jnp.where(slot < 0.0, float(slots), slot).astype(jnp.int32)
        pltpu.sync_copy(slot_lanes, ids)
        sums = jnp.zeros((EXTRA, size), F32)
        acc[...] = jnp.zeros_like(acc)
        for s in range(sectors):
            sums = sums + arrived[s, CAP * share :].astype(F32)
            for c in range(CAP):
                slot = ids[s, c]
                acc[slot] = acc[slot] + arrived[s, c * share : (c + 1) * share].astype(F32)
        sums = jnp.sum(sums, axis=1, keepdims=True)
        total_of = [sums[j : j + 1] for j in range(k)]
        new_state[...] = state[...]

        def gram(i, j):
            row = 8 + 4 * max(i, j) + min(i, j)
            return state[row : row + 1, 0:1]

        def keep(row, value):
            new_state[row : row + 1] = jnp.broadcast_to(value, (1, size))

        project = total_of[: k - 1]
        length = total_of[k - 1]
        crossed = []
        for i in range(k - 1):
            mixed = jnp.zeros((1, 1), F32)
            for j in range(k - 1):
                mixed = mixed + gram(i, j) * project[j]
            crossed.append(mixed)
            length = length + project[i] * (mixed - 2.0 * project[i])
        length = jnp.maximum(length, 0.0)
        scale = 1.0 / jnp.sqrt(length + 1e-6)
        keep(4, scale)
        for j in range(k - 1):
            keep(5 + j, project[j])
            keep(8 + 4 * (k - 1) + j, scale * (project[j] - crossed[j]))
        keep(8 + 4 * (k - 1) + k - 1, length * scale * scale)
        first_row = meta[ROW_POS, 0] * share
        for b in range(slots):
            value = jnp.where(mask_of(meta, b, slots, (share, size), first_row), acc[b], 0.0)
            direction = vector[b]
            for j in range(k - 1):
                value = value - project[j] * images[j][b]
                direction = direction - project[j] * bases[j][b]
            value = value * scale
            direction = direction * scale
            image[b] = value
            basis[b] = direction
            message[b] = value.astype(BF)

    return call(
        body,
        "image",
        [SMEM] + [VMEM] * (3 + 2 * (k - 1)),
        (
            out((slots, share, size), F32),
            out((slots, share, size), F32),
            out((slots, share, size), BF),
            out((24, size), F32),
        ),
        [
            pltpu.VMEM((slots + 1, share, size), F32),
            pltpu.VMEM((sectors, size), jnp.int32),
            pltpu.SMEM((sectors, size), jnp.int32),
        ],
    )


def gather_kernel(slots, size, share, chips):
    def body(*refs):
        for k in range(chips):
            refs[chips][k] = refs[k][...]

    return call(body, "gather", [VMEM] * chips, out((chips, slots, share, size), BF))


def weigh_kernel(k, slots, size, share, sectors, chips):
    def body(meta, mine, other, vector, state, *refs):
        bases = refs[: k - 1]
        image, basis, message = refs[k - 1 :]
        x = meta[ROW_POS, 1]
        c = meta[ROW_POS, 2]
        for j in range(chips):
            origin = 2 * lax.rem(x + chips - j, chips)
            near = pl.multiple_of((origin + c) * share, share)
            far = pl.multiple_of((origin + 1 - c) * share, share)
            image[:, pl.ds(near, share)] = mine[j]
            image[:, pl.ds(far, share)] = other[j]
        scale = state[4:5]
        project = [state[5 + j : 6 + j] for j in range(k - 1)]

        def step(b, acc):
            direction = vector[b]
            for j in range(k - 1):
                direction = direction - project[j] * bases[j][b]
            direction = direction * scale
            basis[b] = direction
            return acc + fold(direction * image[b].astype(F32))

        acc = lax.fori_loop(0, slots, step, jnp.zeros((8, size), F32), unroll=2)
        message[...] = jnp.broadcast_to(total(acc)[None], (sectors, 1, size))

    return call(
        body,
        "weigh",
        [SMEM] + [VMEM] * (3 + k),
        (
            out((slots, size, size), BF),
            out((slots, size, size), F32),
            out((sectors, 1, size), F32),
        ),
    )


def correct_kernel(k, slots, size, share, sectors, last):
    def body(meta, thetas, whole_image, whole_basis, shift, image, basis, state, *refs):
        bases = refs[: k - 1]
        if last:
            corrected, sums, new_state = refs[k - 1 :]
        else:
            whole, xin, corrected, sums, new_state = refs[k - 1 :]
        theta = jnp.sum(thetas[...].reshape(sectors, size), axis=0, keepdims=True)
        new_state[...] = state[...]
        new_state[k - 1 : k] = theta
        first_row = pl.multiple_of(meta[ROW_POS, 0] * share, share)

        def residual(mask, value, direction, moved):
            bottom = jnp.maximum(jnp.abs(moved - theta), 1.0)
            return jnp.where(mask, (value - theta * direction) / bottom, 0.0)

        def step(b, carry):
            direction = whole_basis[b]
            value = residual(
                mask_of(meta, b, slots, (size, size), 0),
                whole_image[b].astype(F32),
                direction,
                shift[b],
            )
            if not last:
                whole[b] = value
                xin[b] = value.astype(BF)
            corrected[b] = residual(
                mask_of(meta, b, slots, (share, size), first_row),
                image[b],
                basis[b],
                shift[b, pl.ds(first_row, share)],
            )
            others = [bases[j][b] for j in range(k - 1)] + [direction, value]
            return tuple(a + fold(value * o) for a, o in zip(carry, others))

        carry = lax.fori_loop(
            0, slots, step, tuple(jnp.zeros((8, size), F32) for _ in range(k + 1)), unroll=2
        )
        if last:
            line = lax.broadcasted_iota(jnp.int32, (EXTRA, size), 0)
            tail = jnp.zeros((EXTRA, size), F32)
            for j in range(k + 1):
                tail = jnp.where(line == j, total(carry[j]), tail)
            sums[...] = jnp.broadcast_to(tail[None], (sectors, EXTRA, size))
        else:
            tail = jnp.zeros((EXTRA, size), F32)
            for j in range(k + 1):
                tail = tail + three_parts(total(carry[j]), j, EXTRA)
            sums[...] = tail

    blocks = out((slots, size, size), F32)
    shapes = [out((slots, share, size), F32), out((EXTRA, size), F32), out((24, size), F32)]
    if last:
        shapes[1] = out((sectors, EXTRA, size), F32)
    else:
        shapes = [blocks, out((slots, size, size), BF)] + shapes
    return call(body, "correct", [SMEM] + [VMEM] * (6 + k), tuple(shapes))


def finish_kernel(slots, size, share, sectors):
    k = APPLIES

    def body(sums, vector, state, *refs):
        bases = refs[:k]
        images = refs[k : 2 * k]
        stacked, final, ritz = refs[2 * k :]
        added = jnp.sum(sums[...], axis=0)
        project = [added[j : j + 1] for j in range(k)]
        length = added[k : k + 1]
        for i in range(k):
            mixed = jnp.zeros((1, size), F32)
            for j in range(k):
                row = 8 + 4 * max(i, j) + min(i, j)
                mixed = mixed + state[row : row + 1] * project[j]
            length = length + project[i] * (mixed - 2.0 * project[i])
        scale = 1.0 / jnp.sqrt(jnp.maximum(length, 0.0) + 1e-6)
        for b in range(slots):
            value = vector[b]
            for j in range(k):
                value = value - project[j] * bases[j][b]
            final[b] = value * scale
            for j in range(k):
                stacked[j, b] = images[j][b]
        for j in range(k):
            ritz[j] = jnp.max(state[j : j + 1])

    return call(
        body,
        "finish",
        [VMEM] * (3 + 2 * k),
        (
            out((k, slots, share, size), F32),
            out((slots, share, size), F32),
            out((k,), F32),
        ),
        out_specs=(VMEM, VMEM, SMEM),
    )


def per_device(
    guess,
    diag_shift,
    block_rows,
    block_cols,
    left_env,
    right_env,
    edge_input,
    edge_left,
    edge_right,
    edge_owner,
    edge_slot,
):
    slots, size, _ = guess.shape
    sectors = lax.axis_size("sector")
    terms = lax.axis_size("mpo")
    edges = edge_input.shape[0]
    group = left_env.shape[0]
    share = size // terms
    chips = terms // 2
    place = lax.axis_index("mpo")
    core_swap = [(i, i ^ 1) for i in range(terms)]
    entry = jnp.arange(edges, dtype=jnp.int32)
    meta = jnp.stack(
        [
            edge_input,
            edge_left,
            edge_right,
            edge_owner[:, 0],
            edge_slot,
            jnp.concatenate([block_rows, block_cols]),
            jnp.where(entry == 0, place, jnp.where(entry == 1, place // 2, place % 2)),
        ]
    )

    def over_sector(values):
        return lax.all_to_all(values, "sector", 0, 0, tiled=True)

    def chip_shift(values, k):
        pairs = [(i, (i + 2 * k) % terms) for i in range(terms)]
        return lax.ppermute(values, "mpo", pairs)

    def far(values):
        return pltpu.with_memory_space_constraint(values, pltpu.HBM)

    vector, xin, mine, sums, state, right_near, left_near = start_kernel(slots, size, share, group)(
        meta, far(guess), far(right_env), far(left_env)
    )
    bases, images, whole_bases = [], [], []
    for k in range(1, APPLIES + 1):
        own, send, right_near, left_near = couple_kernel(edges, slots, size, share, group, chips)(
            meta, xin, right_near, left_near
        )
        received = lax.ppermute(send, "mpo", core_swap)
        parts = pair_kernel(edges, size, share, chips)(own, received)
        shifted = [parts[0]] + [chip_shift(parts[j], j) for j in range(1, chips)]
        message = pack_kernel(edges, size, share, sectors)(meta, sums, *shifted)
        arrived = over_sector(message)
        image, basis, outgoing, state = image_kernel(k, slots, size, share, sectors)(
            meta, arrived, mine, state, *bases, *images
        )
        rows = [outgoing, chip_shift(outgoing, 1), None, chip_shift(outgoing, chips - 1)]
        rows[2] = chip_shift(rows[1], 1)
        near_rows = gather_kernel(slots, size, share, chips)(*rows)
        far_rows = lax.ppermute(near_rows, "mpo", core_swap)
        whole_image, whole_basis, parts = weigh_kernel(k, slots, size, share, sectors, chips)(
            meta, near_rows, far_rows, vector, state, *whole_bases
        )
        thetas = over_sector(parts)
        last = k == APPLIES
        result = correct_kernel(k, slots, size, share, sectors, last)(
            meta, thetas, whole_image, whole_basis, diag_shift, image, basis, state, *whole_bases
        )
        if last:
            mine, sums, state = result
        else:
            vector, xin, mine, sums, state = result
            whole_bases.append(whole_basis)
        bases.append(basis)
        images.append(image)
    stacked, final, ritz = finish_kernel(slots, size, share, sectors)(
        over_sector(sums), mine, state, *bases, *images
    )
    return stacked, final, ritz


def solution(mesh):
    return jax.shard_map(
        per_device,
        mesh=mesh,
        in_specs=(
            P("sector", None, None),
            P("sector", None, None),
            P("sector"),
            P("sector"),
            P("mpo", "sector", None, None),
            P("mpo", "sector", None, None),
            P("sector"),
            P("sector"),
            P("sector"),
            P("sector", None),
            P("sector"),
        ),
        out_specs=(P(None, "sector", "mpo", None), P("sector", "mpo", None), P()),
        check_vma=False,
    )
```

```python
import jax
import jax.numpy as jnp
from jax import lax
from jax.experimental import pallas as pl
from jax.experimental.pallas import tpu as pltpu
from jax.sharding import PartitionSpec as P

APPLIES = 3
CAP = 2
EXTRA = 8
ID_ROW = 4
UNROLL = 16
BF = jnp.bfloat16
F32 = jnp.float32
VMEM = pl.BlockSpec(memory_space=pltpu.VMEM)
SMEM = pl.BlockSpec(memory_space=pltpu.SMEM)
FAR = pl.BlockSpec(memory_space=pltpu.HBM)
PIECES = 4


class Meta:
    def __init__(self, ref, edges, slots):
        self.ref, self.edges, self.slots = ref, edges, slots

    def edge(self, column, e):
        return self.ref[column * self.edges + e]

    def rows(self, b):
        return self.ref[5 * self.edges + b]

    def cols(self, b):
        return self.ref[5 * self.edges + self.slots + b]

    def place(self):
        return self.ref[5 * self.edges + 2 * self.slots]


IN, LEFT, RIGHT, OWNER, SLOT = range(5)


def call(body, name, in_specs, out_shape, scratch=(), mib=8, aliases={}, out_specs=None):
    return pl.pallas_call(
        body,
        name=name,
        in_specs=in_specs,
        out_shape=out_shape,
        out_specs=out_specs or jax.tree.map(lambda _: VMEM, out_shape),
        input_output_aliases=aliases,
        scratch_shapes=scratch,
        compiler_params=pltpu.CompilerParams(vmem_limit_bytes=mib << 20),
    )


def out(shape, dtype):
    return jax.ShapeDtypeStruct(shape, dtype)


def total(values):
    return jnp.sum(jnp.sum(values, axis=0, keepdims=True), axis=1, keepdims=True)


def fold(values):
    return jnp.sum(values.reshape(-1, 8, values.shape[-1]), axis=0)


def three_parts(value, row, height):
    high = value.astype(BF).astype(F32)
    middle = (value - high).astype(BF).astype(F32)
    low = value - high - middle
    lane = lax.broadcasted_iota(jnp.int32, (height, 128), 1)
    line = lax.broadcasted_iota(jnp.int32, (height, 128), 0)
    spread = jnp.where(lane == 0, high, jnp.where(lane == 1, middle, jnp.where(lane == 2, low, 0.0)))
    return jnp.where(line == row, spread, 0.0)


def mask_of(meta, block, shape, first_row):
    line = lax.broadcasted_iota(jnp.int32, shape, 0) + first_row
    lane = lax.broadcasted_iota(jnp.int32, shape, 1)
    return (line < meta.rows(block)) & (lane < meta.cols(block))


def start_kernel(edges, slots, size, share, group):
    def body(meta, far_guess, right, left, *refs):
        meta = Meta(meta, edges, slots)
        vector, xin, own, sums, state, right_near, left_near, guess, sems, guess_sem = refs
        state[...] = jnp.zeros_like(state)
        first = pltpu.make_async_copy(far_guess, guess, guess_sem)
        first.start()
        copies = []
        for i, (far, near) in enumerate(((right, right_near), (left, left_near))):
            for p in range(PIECES):
                part = pl.ds(p * (group // PIECES), group // PIECES)
                copies.append(pltpu.make_async_copy(far.at[part], near.at[part], sems.at[i, p]))
        for copy in copies:
            copy.start()
        acc = jnp.zeros((8, size), F32)
        first_row = pl.multiple_of(meta.place() * share, share)
        first.wait()
        for b in range(slots):
            value = jnp.where(mask_of(meta, b, (size, size), 0), guess[b], 0.0)
            vector[b] = value
            xin[b] = value.astype(BF)
            acc = acc + fold(value * value)
            mine = guess[b, pl.ds(first_row, share)]
            own[b] = jnp.where(mask_of(meta, b, (share, size), first_row), mine, 0.0)
        sums[...] = three_parts(total(acc), 0, EXTRA)
        for copy in copies:
            copy.wait()

    near = pltpu.VMEM((group, slots, size, size), BF)
    return call(
        body,
        "start",
        [SMEM, FAR, FAR, FAR],
        (
            out((slots, size, size), F32),
            out((slots, size, size), BF),
            out((slots, share, size), F32),
            out((EXTRA, size), F32),
            out((24, size), F32),
            near,
            near,
        ),
        [
            pltpu.VMEM((slots, size, size), F32),
            pltpu.SemaphoreType.DMA((2, PIECES)),
            pltpu.SemaphoreType.DMA,
        ],
    )


def couple_kernel(edges, slots, size, share, group, chips):
    def body(meta, xin, right, left, own, send, *refs):
        meta = Meta(meta, edges, slots)
        tmp = refs[-1]
        x = meta.place() // 2
        c = lax.rem(meta.place(), 2)

        def one(e, u):
            i = meta.edge(IN, e)
            le = meta.edge(LEFT, e)
            re = meta.edge(RIGHT, e)
            value = xin[i]
            acc = None
            for w in range(group):
                half = jnp.dot(value, right[w, re], preferred_element_type=F32).astype(BF)
                term = jnp.dot(left[w, le], half, preferred_element_type=F32)
                acc = term if acc is None else acc + term
            tmp[u] = acc.astype(BF)
            for k in range(chips):
                to = lax.rem(x + k, chips)
                mine = pl.multiple_of((2 * to + c) * share, share)
                other = pl.multiple_of((2 * to + 1 - c) * share, share)
                own[k, e] = tmp[u, pl.ds(mine, share)]
                send[k, e] = tmp[u, pl.ds(other, share)]

        def step(t, carry):
            for u in range(UNROLL):
                one(t * UNROLL + u, u)
            return carry

        lax.fori_loop(0, edges // UNROLL, step, 0)

    shape = out((chips, edges, share, size), BF)
    near = pltpu.VMEM((group, slots, size, size), BF)
    return call(
        body,
        "couple",
        [SMEM, VMEM, VMEM, VMEM],
        (shape, shape, near, near),
        [pltpu.VMEM((UNROLL, size, size), BF)],
        aliases={2: 2, 3: 3},
    )


def pair_kernel(edges, size, share, chips):
    def body(own, received, *parts):
        for k in range(chips):
            parts[k][...] = (own[k].astype(F32) + received[k].astype(F32)).astype(BF)

    return call(
        body, "pair", [VMEM, VMEM], tuple(out((edges, share, size), BF) for _ in range(chips))
    )


def pack_kernel(edges, slots, size, share, sectors, with_ids):
    height = CAP * share + EXTRA

    def body(meta, sums, first, second, third, fourth, message, seen):
        meta = Meta(meta, edges, slots)
        message[...] = jnp.zeros_like(message)
        line = lax.broadcasted_iota(jnp.int32, (EXTRA, size), 0)
        lane = lax.broadcasted_iota(jnp.int32, (EXTRA, size), 1)
        tail = sums[...]
        if with_ids:
            tail = jnp.where((line == ID_ROW) & (lane < CAP), -1.0, tail)
        for s in range(sectors):
            seen[s] = 0
            message[s, CAP * share :] = tail.astype(BF)
        for e in range(edges):
            owner = meta.edge(OWNER, e)
            rank = seen[owner]
            seen[owner] = rank + 1
            value = first[e].astype(F32) + second[e].astype(F32)
            value = value + (third[e].astype(F32) + fourth[e].astype(F32))
            message[owner, pl.ds(pl.multiple_of(rank * share, share), share)] = value.astype(BF)
            if with_ids:
                slot = meta.edge(SLOT, e).astype(F32)
                here = message[owner, CAP * share :].astype(F32)
                here = jnp.where((line == ID_ROW) & (lane == rank), slot, here)
                message[owner, CAP * share :] = here.astype(BF)

    return call(
        body,
        "pack",
        [SMEM] + [VMEM] * 5,
        out((sectors, height, size), BF),
        [pltpu.SMEM((sectors,), jnp.int32)],
    )


def image_kernel(k, edges, slots, size, share, sectors):
    def body(meta, arrived, vector, state, *refs):
        meta = Meta(meta, edges, slots)
        bases = refs[: k - 1]
        images = refs[k - 1 : 2 * k - 2]
        if k == 1:
            image, basis, message, new_state, ids, acc, slot_lanes, wide_ids = refs
            line = lax.broadcasted_iota(jnp.int32, (EXTRA, size), 0)
            for s in range(sectors):
                tail = arrived[s, CAP * share :].astype(F32)
                slot = jnp.sum(jnp.where(line == ID_ROW, tail, 0.0), axis=0, keepdims=True)
                slot = jnp.where(slot < 0.0, float(slots), slot)
                slot_lanes[s : s + 1] = slot.astype(jnp.int32)
            pltpu.sync_copy(slot_lanes, wide_ids)
            for s in range(sectors):
                for c in range(CAP):
                    ids[s * CAP + c] = wide_ids[s, c]
        else:
            ids, image, basis, message, new_state, acc = refs[2 * k - 2 :]
        sums = jnp.zeros((EXTRA, size), F32)
        acc[...] = jnp.zeros_like(acc)
        for s in range(sectors):
            sums = sums + arrived[s, CAP * share :].astype(F32)
            for c in range(CAP):
                slot = ids[s * CAP + c]
                acc[slot] = acc[slot] + arrived[s, c * share : (c + 1) * share].astype(F32)
        sums = jnp.sum(sums, axis=1, keepdims=True)
        total_of = [sums[j : j + 1] for j in range(k)]
        new_state[...] = state[...]

        def gram(i, j):
            row = 8 + 4 * max(i, j) + min(i, j)
            return state[row : row + 1, 0:1]

        def keep(row, value):
            new_state[row : row + 1] = jnp.broadcast_to(value, (1, size))

        project = total_of[: k - 1]
        length = total_of[k - 1]
        crossed = []
        for i in range(k - 1):
            mixed = jnp.zeros((1, 1), F32)
            for j in range(k - 1):
                mixed = mixed + gram(i, j) * project[j]
            crossed.append(mixed)
            length = length + project[i] * (mixed - 2.0 * project[i])
        length = jnp.maximum(length, 0.0)
        scale = 1.0 / jnp.sqrt(length + 1e-6)
        keep(4, scale)
        for j in range(k - 1):
            keep(5 + j, project[j])
            keep(8 + 4 * (k - 1) + j, scale * (project[j] - crossed[j]))
        keep(8 + 4 * (k - 1) + k - 1, length * scale * scale)
        first_row = meta.place() * share
        for b in range(slots):
            value = jnp.where(mask_of(meta, b, (share, size), first_row), acc[b], 0.0)
            direction = vector[b]
            for j in range(k - 1):
                value = value - project[j] * images[j][b]
                direction = direction - project[j] * bases[j][b]
            value = value * scale
            direction = direction * scale
            image[b] = value
            basis[b] = direction
            message[b] = value.astype(BF)

    rows = (slots, share, size)
    shapes = [out(rows, F32), out(rows, F32), out(rows, BF), out((24, size), F32)]
    specs = [VMEM] * 4
    scratch = [pltpu.VMEM((slots + 1, share, size), F32)]
    if k == 1:
        shapes.append(out((sectors * CAP,), jnp.int32))
        specs.append(SMEM)
        scratch.append(pltpu.VMEM((sectors, size), jnp.int32))
        scratch.append(pltpu.SMEM((sectors, size), jnp.int32))
    return call(
        body,
        "image",
        [SMEM] + [VMEM] * (3 + 2 * (k - 1)) + ([SMEM] if k > 1 else []),
        tuple(shapes),
        scratch,
        out_specs=tuple(specs),
    )


def gather_kernel(slots, size, share, chips):
    def body(*refs):
        for k in range(chips):
            refs[chips][k] = refs[k][...]

    return call(body, "gather", [VMEM] * chips, out((chips, slots, share, size), BF))


def weigh_kernel(k, edges, slots, size, share, sectors, chips):
    def body(meta, mine, other, vector, state, *refs):
        meta = Meta(meta, edges, slots)
        bases = refs[: k - 1]
        image, basis, message = refs[k - 1 :]
        x = meta.place() // 2
        c = lax.rem(meta.place(), 2)
        for j in range(chips):
            origin = 2 * lax.rem(x + chips - j, chips)
            near = pl.multiple_of((origin + c) * share, share)
            far = pl.multiple_of((origin + 1 - c) * share, share)
            image[:, pl.ds(near, share)] = mine[j]
            image[:, pl.ds(far, share)] = other[j]
        scale = state[4:5]
        project = [state[5 + j : 6 + j] for j in range(k - 1)]

        def step(b, acc):
            direction = vector[b]
            for j in range(k - 1):
                direction = direction - project[j] * bases[j][b]
            direction = direction * scale
            basis[b] = direction
            return acc + fold(direction * image[b].astype(F32))

        acc = lax.fori_loop(0, slots, step, jnp.zeros((8, size), F32), unroll=2)
        message[...] = jnp.broadcast_to(total(acc)[None], (sectors, 1, size))

    return call(
        body,
        "weigh",
        [SMEM] + [VMEM] * (3 + k),
        (
            out((slots, size, size), BF),
            out((slots, size, size), F32),
            out((sectors, 1, size), F32),
        ),
    )


def correct_kernel(k, edges, slots, size, share, sectors, last):
    def body(meta, thetas, whole_image, whole_basis, shift, image, basis, state, *refs):
        meta = Meta(meta, edges, slots)
        bases = refs[: k - 1]
        if last:
            corrected, sums, new_state = refs[k - 1 :]
        else:
            whole, xin, corrected, sums, new_state = refs[k - 1 :]
        theta = jnp.sum(thetas[...].reshape(sectors, size), axis=0, keepdims=True)
        new_state[...] = state[...]
        new_state[k - 1 : k] = theta
        first_row = pl.multiple_of(meta.place() * share, share)

        def residual(mask, value, direction, moved):
            bottom = jnp.maximum(jnp.abs(moved - theta), 1.0)
            return jnp.where(mask, (value - theta * direction) / bottom, 0.0)

        def step(b, carry):
            direction = whole_basis[b]
            value = residual(
                mask_of(meta, b, (size, size), 0),
                whole_image[b].astype(F32),
                direction,
                shift[b],
            )
            if not last:
                whole[b] = value
                xin[b] = value.astype(BF)
            corrected[b] = residual(
                mask_of(meta, b, (share, size), first_row),
                image[b],
                basis[b],
                shift[b, pl.ds(first_row, share)],
            )
            others = [bases[j][b] for j in range(k - 1)] + [direction, value]
            return tuple(a + fold(value * o) for a, o in zip(carry, others))

        carry = lax.fori_loop(
            0, slots, step, tuple(jnp.zeros((8, size), F32) for _ in range(k + 1)), unroll=2
        )
        if last:
            line = lax.broadcasted_iota(jnp.int32, (EXTRA, size), 0)
            tail = jnp.zeros((EXTRA, size), F32)
            for j in range(k + 1):
                tail = jnp.where(line == j, total(carry[j]), tail)
            sums[...] = jnp.broadcast_to(tail[None], (sectors, EXTRA, size))
        else:
            tail = jnp.zeros((EXTRA, size), F32)
            for j in range(k + 1):
                tail = tail + three_parts(total(carry[j]), j, EXTRA)
            sums[...] = tail

    blocks = out((slots, size, size), F32)
    shapes = [out((slots, share, size), F32), out((EXTRA, size), F32), out((24, size), F32)]
    if last:
        shapes[1] = out((sectors, EXTRA, size), F32)
    else:
        shapes = [blocks, out((slots, size, size), BF)] + shapes
    return call(body, "correct", [SMEM] + [VMEM] * (6 + k), tuple(shapes))


def finish_kernel(slots, size, share, sectors):
    k = APPLIES

    def body(sums, vector, state, *refs):
        bases = refs[:k]
        images = refs[k : 2 * k]
        stacked, final, ritz = refs[2 * k :]
        added = jnp.sum(sums[...], axis=0)
        project = [added[j : j + 1] for j in range(k)]
        length = added[k : k + 1]
        for i in range(k):
            mixed = jnp.zeros((1, size), F32)
            for j in range(k):
                row = 8 + 4 * max(i, j) + min(i, j)
                mixed = mixed + state[row : row + 1] * project[j]
            length = length + project[i] * (mixed - 2.0 * project[i])
        scale = 1.0 / jnp.sqrt(jnp.maximum(length, 0.0) + 1e-6)
        for b in range(slots):
            value = vector[b]
            for j in range(k):
                value = value - project[j] * bases[j][b]
            final[b] = value * scale
            for j in range(k):
                stacked[j, b] = images[j][b]
        for j in range(k):
            ritz[j] = jnp.max(state[j : j + 1])

    return call(
        body,
        "finish",
        [VMEM] * (3 + 2 * k),
        (
            out((k, slots, share, size), F32),
            out((slots, share, size), F32),
            out((k,), F32),
        ),
        out_specs=(VMEM, VMEM, SMEM),
    )


def per_device(
    guess,
    diag_shift,
    block_rows,
    block_cols,
    left_env,
    right_env,
    edge_input,
    edge_left,
    edge_right,
    edge_owner,
    edge_slot,
):
    slots, size, _ = guess.shape
    sectors = lax.axis_size("sector")
    terms = lax.axis_size("mpo")
    edges = edge_input.shape[0]
    group = left_env.shape[0]
    share = size // terms
    chips = terms // 2
    place = lax.axis_index("mpo")
    core_swap = [(i, i ^ 1) for i in range(terms)]
    meta = jnp.concatenate(
        [
            edge_input,
            edge_left,
            edge_right,
            edge_owner[:, 0],
            edge_slot,
            block_rows,
            block_cols,
            place[None].astype(jnp.int32),
        ]
    )

    def over_sector(values):
        return lax.all_to_all(values, "sector", 0, 0, tiled=True)

    def chip_shift(values, k):
        pairs = [(i, (i + 2 * k) % terms) for i in range(terms)]
        return lax.ppermute(values, "mpo", pairs)

    def far(values):
        return pltpu.with_memory_space_constraint(values, pltpu.HBM)

    vector, xin, mine, sums, state, right_near, left_near = start_kernel(edges, slots, size, share, group)(
        meta, far(guess), far(right_env), far(left_env)
    )
    bases, images, whole_bases, ids = [], [], [], []
    for k in range(1, APPLIES + 1):
        own, send, right_near, left_near = couple_kernel(edges, slots, size, share, group, chips)(
            meta, xin, right_near, left_near
        )
        received = lax.ppermute(send, "mpo", core_swap)
        parts = pair_kernel(edges, size, share, chips)(own, received)
        shifted = [parts[0]] + [chip_shift(parts[j], j) for j in range(1, chips)]
        message = pack_kernel(edges, slots, size, share, sectors, k == 1)(meta, sums, *shifted)
        arrived = over_sector(message)
        result = image_kernel(k, edges, slots, size, share, sectors)(
            meta, arrived, mine, state, *bases, *images, *ids
        )
        image, basis, outgoing, state = result[:4]
        if k == 1:
            ids = result[4:]
        rows = [outgoing] + [chip_shift(outgoing, j) for j in range(1, chips)]
        near_rows = gather_kernel(slots, size, share, chips)(*rows)
        far_rows = lax.ppermute(near_rows, "mpo", core_swap)
        whole_image, whole_basis, parts = weigh_kernel(
            k, edges, slots, size, share, sectors, chips
        )(
            meta, near_rows, far_rows, vector, state, *whole_bases
        )
        thetas = over_sector(parts)
        last = k == APPLIES
        result = correct_kernel(k, edges, slots, size, share, sectors, last)(
            meta, thetas, whole_image, whole_basis, diag_shift, image, basis, state, *whole_bases
        )
        if last:
            mine, sums, state = result
        else:
            vector, xin, mine, sums, state = result
            whole_bases.append(whole_basis)
        bases.append(basis)
        images.append(image)
    stacked, final, ritz = finish_kernel(slots, size, share, sectors)(
        over_sector(sums), mine, state, *bases, *images
    )
    return stacked, final, ritz


def solution(mesh):
    return jax.shard_map(
        per_device,
        mesh=mesh,
        in_specs=(
            P("sector", None, None),
            P("sector", None, None),
            P("sector"),
            P("sector"),
            P("mpo", "sector", None, None),
            P("mpo", "sector", None, None),
            P("sector"),
            P("sector"),
            P("sector"),
            P("sector", None),
            P("sector"),
        ),
        out_specs=(P(None, "sector", "mpo", None), P("sector", "mpo", None), P()),
        check_vma=False,
    )
```

```python
import jax
import jax.numpy as jnp
from jax import lax
from jax.experimental import pallas as pl
from jax.experimental.pallas import tpu as pltpu
from jax.sharding import PartitionSpec as P

APPLIES = 3
CAP = 2
EXTRA = 8
ID_ROW = 4
UNROLL = 16
BF = jnp.bfloat16
F32 = jnp.float32
VMEM = pl.BlockSpec(memory_space=pltpu.VMEM)
SMEM = pl.BlockSpec(memory_space=pltpu.SMEM)
FAR = pl.BlockSpec(memory_space=pltpu.HBM)
PIECES = 4


class Meta:
    def __init__(self, ref, edges, slots):
        self.ref, self.edges, self.slots = ref, edges, slots

    def edge(self, column, e):
        return self.ref[column * self.edges + e]

    def rows(self, b):
        return self.ref[5 * self.edges + b]

    def cols(self, b):
        return self.ref[5 * self.edges + self.slots + b]

    def place(self):
        return self.ref[5 * self.edges + 2 * self.slots]


IN, LEFT, RIGHT, OWNER, SLOT = range(5)


def call(body, name, in_specs, out_shape, scratch=(), mib=8, aliases={}, out_specs=None):
    return pl.pallas_call(
        body,
        name=name,
        in_specs=in_specs,
        out_shape=out_shape,
        out_specs=out_specs or jax.tree.map(lambda _: VMEM, out_shape),
        input_output_aliases=aliases,
        scratch_shapes=scratch,
        compiler_params=pltpu.CompilerParams(vmem_limit_bytes=mib << 20),
    )


def out(shape, dtype):
    return jax.ShapeDtypeStruct(shape, dtype)


def total(values):
    return jnp.sum(jnp.sum(values, axis=0, keepdims=True), axis=1, keepdims=True)


def fold(values):
    return jnp.sum(values.reshape(-1, 8, values.shape[-1]), axis=0)


def three_parts(value, row, height):
    high = value.astype(BF).astype(F32)
    middle = (value - high).astype(BF).astype(F32)
    low = value - high - middle
    lane = lax.broadcasted_iota(jnp.int32, (height, 128), 1)
    line = lax.broadcasted_iota(jnp.int32, (height, 128), 0)
    spread = jnp.where(lane == 0, high, jnp.where(lane == 1, middle, jnp.where(lane == 2, low, 0.0)))
    return jnp.where(line == row, spread, 0.0)


def mask_of(meta, block, shape, first_row):
    line = lax.broadcasted_iota(jnp.int32, shape, 0) + first_row
    lane = lax.broadcasted_iota(jnp.int32, shape, 1)
    return (line < meta.rows(block)) & (lane < meta.cols(block))


def start_kernel(edges, slots, size, share, group):
    def body(meta, far_guess, right, left, *refs):
        meta = Meta(meta, edges, slots)
        vector, xin, own, sums, state, right_near, left_near, guess, sems, guess_sem = refs
        state[...] = jnp.zeros_like(state)
        first = pltpu.make_async_copy(far_guess, guess, guess_sem)
        first.start()
        copies = []
        for i, (far, near) in enumerate(((right, right_near), (left, left_near))):
            for p in range(PIECES):
                part = pl.ds(p * (group // PIECES), group // PIECES)
                copies.append(pltpu.make_async_copy(far.at[part], near.at[part], sems.at[i, p]))
        for copy in copies:
            copy.start()
        acc = jnp.zeros((8, size), F32)
        first_row = pl.multiple_of(meta.place() * share, share)
        first.wait()
        for b in range(slots):
            value = jnp.where(mask_of(meta, b, (size, size), 0), guess[b], 0.0)
            vector[b] = value
            xin[b] = value.astype(BF)
            acc = acc + fold(value * value)
            mine = guess[b, pl.ds(first_row, share)]
            own[b] = jnp.where(mask_of(meta, b, (share, size), first_row), mine, 0.0)
        sums[...] = three_parts(total(acc), 0, EXTRA)
        for copy in copies:
            copy.wait()

    near = pltpu.VMEM((group, slots, size, size), BF)
    return call(
        body,
        "start",
        [SMEM, FAR, FAR, FAR],
        (
            out((slots, size, size), F32),
            out((slots, size, size), BF),
            out((slots, share, size), F32),
            out((EXTRA, size), F32),
            out((24, size), F32),
            near,
            near,
        ),
        [
            pltpu.VMEM((slots, size, size), F32),
            pltpu.SemaphoreType.DMA((2, PIECES)),
            pltpu.SemaphoreType.DMA,
        ],
    )


def couple_kernel(edges, slots, size, share, group, chips):
    def body(meta, xin, right, left, own, send, *refs):
        meta = Meta(meta, edges, slots)
        tmp = refs[-1]
        x = meta.place() // 2
        c = lax.rem(meta.place(), 2)

        def one(e, u):
            i = meta.edge(IN, e)
            le = meta.edge(LEFT, e)
            re = meta.edge(RIGHT, e)
            value = xin[i]
            acc = None
            for w in range(group):
                half = jnp.dot(value, right[w, re], preferred_element_type=F32).astype(BF)
                term = jnp.dot(left[w, le], half, preferred_element_type=F32)
                acc = term if acc is None else acc + term
            tmp[u] = acc.astype(BF)
            for k in range(chips):
                to = lax.rem(x + k, chips)
                mine = pl.multiple_of((2 * to + c) * share, share)
                other = pl.multiple_of((2 * to + 1 - c) * share, share)
                own[k, e] = tmp[u, pl.ds(mine, share)]
                send[k, e] = tmp[u, pl.ds(other, share)]

        def step(t, carry):
            for u in range(UNROLL):
                one(t * UNROLL + u, u)
            return carry

        lax.fori_loop(0, edges // UNROLL, step, 0)

    shape = out((chips, edges, share, size), BF)
    near = pltpu.VMEM((group, slots, size, size), BF)
    return call(
        body,
        "couple",
        [SMEM, VMEM, VMEM, VMEM],
        (shape, shape, near, near),
        [pltpu.VMEM((UNROLL, size, size), BF)],
        aliases={2: 2, 3: 3},
    )


def pair_kernel(edges, size, share, chips):
    def body(own, received, *parts):
        for k in range(chips):
            parts[k][...] = (own[k].astype(F32) + received[k].astype(F32)).astype(BF)

    return call(
        body, "pair", [VMEM, VMEM], tuple(out((edges, share, size), BF) for _ in range(chips))
    )


def pack_kernel(edges, slots, size, share, sectors, with_ids):
    height = CAP * share + EXTRA

    def body(meta, sums, first, second, third, fourth, message, seen):
        meta = Meta(meta, edges, slots)
        message[...] = jnp.zeros_like(message)
        line = lax.broadcasted_iota(jnp.int32, (EXTRA, size), 0)
        lane = lax.broadcasted_iota(jnp.int32, (EXTRA, size), 1)
        tail = sums[...]
        if with_ids:
            tail = jnp.where((line == ID_ROW) & (lane < CAP), -1.0, tail)
        for s in range(sectors):
            seen[s] = 0
            message[s, CAP * share :] = tail.astype(BF)
        for e in range(edges):
            owner = meta.edge(OWNER, e)
            rank = seen[owner]
            seen[owner] = rank + 1
            value = first[e].astype(F32) + second[e].astype(F32)
            value = value + (third[e].astype(F32) + fourth[e].astype(F32))
            message[owner, pl.ds(pl.multiple_of(rank * share, share), share)] = value.astype(BF)
            if with_ids:
                slot = meta.edge(SLOT, e).astype(F32)
                here = message[owner, CAP * share :].astype(F32)
                here = jnp.where((line == ID_ROW) & (lane == rank), slot, here)
                message[owner, CAP * share :] = here.astype(BF)

    return call(
        body,
        "pack",
        [SMEM] + [VMEM] * 5,
        out((sectors, height, size), BF),
        [pltpu.SMEM((sectors,), jnp.int32)],
    )


def image_kernel(k, edges, slots, size, share, sectors, devices):
    last = k == APPLIES

    def body(meta, arrived, vector, state, *refs):
        meta = Meta(meta, edges, slots)
        bases = refs[: k - 1]
        images = refs[k - 1 : 2 * k - 2]
        if k == 1:
            image, basis, message, new_state, ids, acc, slot_lanes, wide_ids = refs
            line = lax.broadcasted_iota(jnp.int32, (EXTRA, size), 0)
            for s in range(sectors):
                tail = arrived[s, CAP * share :].astype(F32)
                slot = jnp.sum(jnp.where(line == ID_ROW, tail, 0.0), axis=0, keepdims=True)
                slot = jnp.where(slot < 0.0, float(slots), slot)
                slot_lanes[s : s + 1] = slot.astype(jnp.int32)
            pltpu.sync_copy(slot_lanes, wide_ids)
            for s in range(sectors):
                for c in range(CAP):
                    ids[s * CAP + c] = wide_ids[s, c]
        else:
            ids, image, basis, message, new_state, acc = refs[2 * k - 2 :]
        sums = jnp.zeros((EXTRA, size), F32)
        acc[...] = jnp.zeros_like(acc)
        for s in range(sectors):
            sums = sums + arrived[s, CAP * share :].astype(F32)
            for c in range(CAP):
                slot = ids[s * CAP + c]
                acc[slot] = acc[slot] + arrived[s, c * share : (c + 1) * share].astype(F32)
        sums = jnp.sum(sums, axis=1, keepdims=True)
        total_of = [sums[j : j + 1] for j in range(k)]
        new_state[...] = state[...]

        def gram(i, j):
            row = 8 + 4 * max(i, j) + min(i, j)
            return state[row : row + 1, 0:1]

        def keep(row, value):
            new_state[row : row + 1] = jnp.broadcast_to(value, (1, size))

        project = total_of[: k - 1]
        length = total_of[k - 1]
        crossed = []
        for i in range(k - 1):
            mixed = jnp.zeros((1, 1), F32)
            for j in range(k - 1):
                mixed = mixed + gram(i, j) * project[j]
            crossed.append(mixed)
            length = length + project[i] * (mixed - 2.0 * project[i])
        length = jnp.maximum(length, 0.0)
        scale = 1.0 / jnp.sqrt(length + 1e-6)
        keep(4, scale)
        for j in range(k - 1):
            keep(5 + j, project[j])
            keep(8 + 4 * (k - 1) + j, scale * (project[j] - crossed[j]))
        keep(8 + 4 * (k - 1) + k - 1, length * scale * scale)
        first_row = meta.place() * share
        theta = jnp.zeros((8, size), F32)
        for b in range(slots):
            value = jnp.where(mask_of(meta, b, (share, size), first_row), acc[b], 0.0)
            direction = vector[b]
            for j in range(k - 1):
                value = value - project[j] * images[j][b]
                direction = direction - project[j] * bases[j][b]
            value = value * scale
            direction = direction * scale
            image[b] = value
            basis[b] = direction
            if last:
                theta = theta + fold(value * direction)
            else:
                message[b] = value.astype(BF)
        if last:
            message[...] = jnp.broadcast_to(total(theta)[None], (devices, 1, size))

    rows = (slots, share, size)
    sent = out((devices, 1, size), F32) if last else out(rows, BF)
    shapes = [out(rows, F32), out(rows, F32), sent, out((24, size), F32)]
    specs = [VMEM] * 4
    scratch = [pltpu.VMEM((slots + 1, share, size), F32)]
    if k == 1:
        shapes.append(out((sectors * CAP,), jnp.int32))
        specs.append(SMEM)
        scratch.append(pltpu.VMEM((sectors, size), jnp.int32))
        scratch.append(pltpu.SMEM((sectors, size), jnp.int32))
    return call(
        body,
        "image",
        [SMEM] + [VMEM] * (3 + 2 * (k - 1)) + ([SMEM] if k > 1 else []),
        tuple(shapes),
        scratch,
        out_specs=tuple(specs),
    )


def gather_kernel(slots, size, share, chips):
    def body(*refs):
        for k in range(chips):
            refs[chips][k] = refs[k][...]

    return call(body, "gather", [VMEM] * chips, out((chips, slots, share, size), BF))


def weigh_kernel(k, edges, slots, size, share, sectors, chips):
    def body(meta, mine, other, vector, state, *refs):
        meta = Meta(meta, edges, slots)
        bases = refs[: k - 1]
        image, basis, message = refs[k - 1 :]
        x = meta.place() // 2
        c = lax.rem(meta.place(), 2)
        for j in range(chips):
            origin = 2 * lax.rem(x + chips - j, chips)
            near = pl.multiple_of((origin + c) * share, share)
            far = pl.multiple_of((origin + 1 - c) * share, share)
            image[:, pl.ds(near, share)] = mine[j]
            image[:, pl.ds(far, share)] = other[j]
        scale = state[4:5]
        project = [state[5 + j : 6 + j] for j in range(k - 1)]

        def step(b, acc):
            direction = vector[b]
            for j in range(k - 1):
                direction = direction - project[j] * bases[j][b]
            direction = direction * scale
            basis[b] = direction
            return acc + fold(direction * image[b].astype(F32))

        acc = lax.fori_loop(0, slots, step, jnp.zeros((8, size), F32), unroll=2)
        message[...] = jnp.broadcast_to(total(acc)[None], (sectors, 1, size))

    return call(
        body,
        "weigh",
        [SMEM] + [VMEM] * (3 + k),
        (
            out((slots, size, size), BF),
            out((slots, size, size), F32),
            out((sectors, 1, size), F32),
        ),
    )


def residual(mask, value, direction, moved, theta):
    bottom = jnp.maximum(jnp.abs(moved - theta), 1.0)
    return jnp.where(mask, (value - theta * direction) / bottom, 0.0)


def correct_kernel(k, edges, slots, size, share):
    def body(meta, thetas, whole_image, whole_basis, shift, image, basis, state, *refs):
        meta = Meta(meta, edges, slots)
        bases = refs[: k - 1]
        whole, xin, corrected, sums, new_state = refs[k - 1 :]
        theta = jnp.sum(thetas[...], axis=0)
        new_state[...] = state[...]
        new_state[k - 1 : k] = theta
        first_row = pl.multiple_of(meta.place() * share, share)

        def step(b, carry):
            direction = whole_basis[b]
            value = residual(
                mask_of(meta, b, (size, size), 0),
                whole_image[b].astype(F32),
                direction,
                shift[b],
                theta,
            )
            whole[b] = value
            xin[b] = value.astype(BF)
            corrected[b] = residual(
                mask_of(meta, b, (share, size), first_row),
                image[b],
                basis[b],
                shift[b, pl.ds(first_row, share)],
                theta,
            )
            others = [bases[j][b] for j in range(k - 1)] + [direction, value]
            return tuple(a + fold(value * o) for a, o in zip(carry, others))

        carry = lax.fori_loop(
            0, slots, step, tuple(jnp.zeros((8, size), F32) for _ in range(k + 1)), unroll=2
        )
        tail = jnp.zeros((EXTRA, size), F32)
        for j in range(k + 1):
            tail = tail + three_parts(total(carry[j]), j, EXTRA)
        sums[...] = tail

    return call(
        body,
        "correct",
        [SMEM] + [VMEM] * (6 + k),
        (
            out((slots, size, size), F32),
            out((slots, size, size), BF),
            out((slots, share, size), F32),
            out((EXTRA, size), F32),
            out((24, size), F32),
        ),
    )


def correct_rows_kernel(edges, slots, size, share, devices):
    k = APPLIES

    def body(meta, thetas, shift, image, state, *refs):
        meta = Meta(meta, edges, slots)
        bases = refs[:k]
        corrected, message, new_state = refs[k:]
        theta = jnp.sum(thetas[...], axis=0)
        new_state[...] = state[...]
        new_state[k - 1 : k] = theta
        first_row = pl.multiple_of(meta.place() * share, share)
        carry = [jnp.zeros((8, size), F32) for _ in range(k + 1)]
        for b in range(slots):
            value = residual(
                mask_of(meta, b, (share, size), first_row),
                image[b],
                bases[k - 1][b],
                shift[b, pl.ds(first_row, share)],
                theta,
            )
            corrected[b] = value
            others = [bases[j][b] for j in range(k)] + [value]
            carry = [a + fold(value * o) for a, o in zip(carry, others)]
        lane = lax.broadcasted_iota(jnp.int32, (1, size), 1)
        row = jnp.zeros((1, size), F32)
        for j in range(k + 1):
            row = jnp.where(lane == j, total(carry[j]), row)
        message[...] = jnp.broadcast_to(row[None], (devices, 1, size))

    return call(
        body,
        "correct_rows",
        [SMEM] + [VMEM] * (4 + k),
        (
            out((slots, share, size), F32),
            out((devices, 1, size), F32),
            out((24, size), F32),
        ),
    )


def finish_kernel(slots, size, share):
    k = APPLIES

    def body(sums, vector, state, *refs):
        bases = refs[:k]
        images = refs[k : 2 * k]
        stacked, final, ritz = refs[2 * k :]
        added = jnp.sum(sums[...], axis=0)
        lane = lax.broadcasted_iota(jnp.int32, (1, size), 1)
        totals = [total(jnp.where(lane == j, added, 0.0)) for j in range(k + 1)]
        project = totals[:k]
        length = totals[k]
        for i in range(k):
            mixed = jnp.zeros((1, 1), F32)
            for j in range(k):
                row = 8 + 4 * max(i, j) + min(i, j)
                mixed = mixed + state[row : row + 1, 0:1] * project[j]
            length = length + project[i] * (mixed - 2.0 * project[i])
        scale = 1.0 / jnp.sqrt(jnp.maximum(length, 0.0) + 1e-6)
        for b in range(slots):
            value = vector[b]
            for j in range(k):
                value = value - project[j] * bases[j][b]
            final[b] = value * scale
            for j in range(k):
                stacked[j, b] = images[j][b]
        for j in range(k):
            ritz[j] = jnp.max(state[j : j + 1])

    return call(
        body,
        "finish",
        [VMEM] * (3 + 2 * k),
        (
            out((k, slots, share, size), F32),
            out((slots, share, size), F32),
            out((k,), F32),
        ),
        out_specs=(VMEM, VMEM, SMEM),
    )


def per_device(
    guess,
    diag_shift,
    block_rows,
    block_cols,
    left_env,
    right_env,
    edge_input,
    edge_left,
    edge_right,
    edge_owner,
    edge_slot,
):
    slots, size, _ = guess.shape
    sectors = lax.axis_size("sector")
    terms = lax.axis_size("mpo")
    edges = edge_input.shape[0]
    group = left_env.shape[0]
    share = size // terms
    chips = terms // 2
    devices = sectors * terms
    place = lax.axis_index("mpo")
    core_swap = [(i, i ^ 1) for i in range(terms)]
    meta = jnp.concatenate(
        [
            edge_input,
            edge_left,
            edge_right,
            edge_owner[:, 0],
            edge_slot,
            block_rows,
            block_cols,
            place[None].astype(jnp.int32),
        ]
    )

    def over_sector(values):
        return lax.all_to_all(values, "sector", 0, 0, tiled=True)

    def over_all(values):
        return lax.all_to_all(values, ("sector", "mpo"), 0, 0, tiled=True)

    def chip_shift(values, k):
        pairs = [(i, (i + 2 * k) % terms) for i in range(terms)]
        return lax.ppermute(values, "mpo", pairs)

    def far(values):
        return pltpu.with_memory_space_constraint(values, pltpu.HBM)

    vector, xin, mine, sums, state, right_near, left_near = start_kernel(edges, slots, size, share, group)(
        meta, far(guess), far(right_env), far(left_env)
    )
    bases, images, whole_bases, ids = [], [], [], []
    for k in range(1, APPLIES + 1):
        own, send, right_near, left_near = couple_kernel(edges, slots, size, share, group, chips)(
            meta, xin, right_near, left_near
        )
        received = lax.ppermute(send, "mpo", core_swap)
        parts = pair_kernel(edges, size, share, chips)(own, received)
        shifted = [parts[0]] + [chip_shift(parts[j], j) for j in range(1, chips)]
        message = pack_kernel(edges, slots, size, share, sectors, k == 1)(meta, sums, *shifted)
        arrived = over_sector(message)
        result = image_kernel(k, edges, slots, size, share, sectors, devices)(
            meta, arrived, mine, state, *bases, *images, *ids
        )
        image, basis, outgoing, state = result[:4]
        bases.append(basis)
        images.append(image)
        if k == 1:
            ids = result[4:]
        if k == APPLIES:
            break
        rows = [outgoing] + [chip_shift(outgoing, j) for j in range(1, chips)]
        near_rows = gather_kernel(slots, size, share, chips)(*rows)
        far_rows = lax.ppermute(near_rows, "mpo", core_swap)
        whole_image, whole_basis, parts = weigh_kernel(
            k, edges, slots, size, share, sectors, chips
        )(meta, near_rows, far_rows, vector, state, *whole_bases)
        vector, xin, mine, sums, state = correct_kernel(k, edges, slots, size, share)(
            meta,
            over_sector(parts),
            whole_image,
            whole_basis,
            diag_shift,
            image,
            basis,
            state,
            *whole_bases,
        )
        whole_bases.append(whole_basis)
    mine, parts, state = correct_rows_kernel(edges, slots, size, share, devices)(
        meta, over_all(outgoing), diag_shift, image, state, *bases
    )
    return finish_kernel(slots, size, share)(over_all(parts), mine, state, *bases, *images)


def solution(mesh):
    return jax.shard_map(
        per_device,
        mesh=mesh,
        in_specs=(
            P("sector", None, None),
            P("sector", None, None),
            P("sector"),
            P("sector"),
            P("mpo", "sector", None, None),
            P("mpo", "sector", None, None),
            P("sector"),
            P("sector"),
            P("sector"),
            P("sector", None),
            P("sector"),
        ),
        out_specs=(P(None, "sector", "mpo", None), P("sector", "mpo", None), P()),
        check_vma=False,
    )
```

```python
import jax
import jax.numpy as jnp
from jax import lax
from jax.experimental import pallas as pl
from jax.experimental.pallas import tpu as pltpu
from jax.sharding import PartitionSpec as P

APPLIES = 3
CAP = 2
EXTRA = 8
ID_ROW = 4
UNROLL = 16
BF = jnp.bfloat16
F32 = jnp.float32
VMEM = pl.BlockSpec(memory_space=pltpu.VMEM)
SMEM = pl.BlockSpec(memory_space=pltpu.SMEM)
FAR = pl.BlockSpec(memory_space=pltpu.HBM)
PIECES = 4


class Meta:
    def __init__(self, ref, edges, slots):
        self.ref, self.edges, self.slots = ref, edges, slots

    def edge(self, column, e):
        return self.ref[column * self.edges + e]

    def rows(self, b):
        return self.ref[5 * self.edges + b]

    def cols(self, b):
        return self.ref[5 * self.edges + self.slots + b]

    def place(self):
        return self.ref[5 * self.edges + 2 * self.slots]


IN, LEFT, RIGHT, OWNER, SLOT = range(5)


def call(body, name, in_specs, out_shape, scratch=(), mib=8, aliases={}, out_specs=None):
    return pl.pallas_call(
        body,
        name=name,
        in_specs=in_specs,
        out_shape=out_shape,
        out_specs=out_specs or jax.tree.map(lambda _: VMEM, out_shape),
        input_output_aliases=aliases,
        scratch_shapes=scratch,
        compiler_params=pltpu.CompilerParams(vmem_limit_bytes=mib << 20),
    )


def out(shape, dtype):
    return jax.ShapeDtypeStruct(shape, dtype)


def total(values):
    return jnp.sum(jnp.sum(values, axis=0, keepdims=True), axis=1, keepdims=True)


def fold(values):
    return jnp.sum(values.reshape(-1, 8, values.shape[-1]), axis=0)


def three_parts(value, row, height):
    high = value.astype(BF).astype(F32)
    middle = (value - high).astype(BF).astype(F32)
    low = value - high - middle
    lane = lax.broadcasted_iota(jnp.int32, (height, 128), 1)
    line = lax.broadcasted_iota(jnp.int32, (height, 128), 0)
    spread = jnp.where(lane == 0, high, jnp.where(lane == 1, middle, jnp.where(lane == 2, low, 0.0)))
    return jnp.where(line == row, spread, 0.0)


def mask_of(meta, block, shape, first_row):
    line = lax.broadcasted_iota(jnp.int32, shape, 0) + first_row
    lane = lax.broadcasted_iota(jnp.int32, shape, 1)
    return (line < meta.rows(block)) & (lane < meta.cols(block))


def couple_rows(meta, chips, share, own, send, tmp, e, u, value):
    x = meta.place() // 2
    c = lax.rem(meta.place(), 2)
    tmp[u] = value.astype(BF)
    for k in range(chips):
        to = lax.rem(x + k, chips)
        mine = pl.multiple_of((2 * to + c) * share, share)
        other = pl.multiple_of((2 * to + 1 - c) * share, share)
        own[k, e] = tmp[u, pl.ds(mine, share)]
        send[k, e] = tmp[u, pl.ds(other, share)]


def add_terms(meta, xin, right, left, e, terms, acc):
    value = xin[meta.edge(IN, e)]
    le = meta.edge(LEFT, e)
    re = meta.edge(RIGHT, e)
    for w in terms:
        half = jnp.dot(value, right[w, re], preferred_element_type=F32).astype(BF)
        term = jnp.dot(left[w, le], half, preferred_element_type=F32)
        acc = term if acc is None else acc + term
    return acc


def unrolled(edges, one):
    def step(t, carry):
        for u in range(UNROLL):
            one(t * UNROLL + u, u)
        return carry

    lax.fori_loop(0, edges // UNROLL, step, 0)


def begin_kernel(edges, slots, size, share, group, chips):
    terms = group // PIECES

    def body(meta, far_guess, right, left, *refs):
        meta = Meta(meta, edges, slots)
        vector, xin, mine, sums, state, right_near, left_near, own, send = refs[:9]
        guess, acc, tmp, sems, guess_sem = refs[9:]
        first = pltpu.make_async_copy(far_guess, guess, guess_sem)
        first.start()
        copies = []
        for p in range(PIECES):
            part = pl.ds(p * terms, terms)
            copies.append(
                [
                    pltpu.make_async_copy(far.at[part], near.at[part], sems.at[i, p])
                    for i, (far, near) in enumerate(((right, right_near), (left, left_near)))
                ]
            )
            for copy in copies[p]:
                copy.start()
        state[...] = jnp.zeros_like(state)
        first_row = pl.multiple_of(meta.place() * share, share)
        first.wait()

        def block(b, squares):
            value = jnp.where(mask_of(meta, b, (size, size), 0), guess[b], 0.0)
            vector[b] = value
            xin[b] = value.astype(BF)
            rows = guess[b, pl.ds(first_row, share)]
            mine[b] = jnp.where(mask_of(meta, b, (share, size), first_row), rows, 0.0)
            return squares + fold(value * value)

        squares = lax.fori_loop(0, slots, block, jnp.zeros((8, size), F32), unroll=4)
        sums[...] = three_parts(total(squares), 0, EXTRA)
        half = PIECES // 2
        for p in range(half):
            for copy in copies[p]:
                copy.wait()

        def early(e, u):
            acc[e] = add_terms(meta, xin, right_near, left_near, e, range(group // 2), None)

        unrolled(edges, early)
        for p in range(half, PIECES):
            for copy in copies[p]:
                copy.wait()

        def late(e, u):
            rest = range(group // 2, group)
            value = add_terms(meta, xin, right_near, left_near, e, rest, acc[e])
            couple_rows(meta, chips, share, own, send, tmp, e, u, value)

        unrolled(edges, late)

    near = pltpu.VMEM((group, slots, size, size), BF)
    shape = out((chips, edges, share, size), BF)
    return call(
        body,
        "begin",
        [SMEM, FAR, FAR, FAR],
        (
            out((slots, size, size), F32),
            out((slots, size, size), BF),
            out((slots, share, size), F32),
            out((EXTRA, size), F32),
            out((24, size), F32),
            near,
            near,
            shape,
            shape,
        ),
        [
            pltpu.VMEM((slots, size, size), F32),
            pltpu.VMEM((edges, size, size), F32),
            pltpu.VMEM((UNROLL, size, size), BF),
            pltpu.SemaphoreType.DMA((2, PIECES)),
            pltpu.SemaphoreType.DMA,
        ],
    )


def couple_kernel(edges, slots, size, share, group, chips):
    def body(meta, xin, right, left, own, send, *refs):
        meta = Meta(meta, edges, slots)
        tmp = refs[-1]

        def one(e, u):
            value = add_terms(meta, xin, right, left, e, range(group), None)
            couple_rows(meta, chips, share, own, send, tmp, e, u, value)

        unrolled(edges, one)

    shape = out((chips, edges, share, size), BF)
    near = pltpu.VMEM((group, slots, size, size), BF)
    return call(
        body,
        "couple",
        [SMEM, VMEM, VMEM, VMEM],
        (shape, shape, near, near),
        [pltpu.VMEM((UNROLL, size, size), BF)],
        aliases={2: 2, 3: 3},
    )


def pair_kernel(edges, size, share, chips):
    def body(own, received, *parts):
        for k in range(chips):
            parts[k][...] = (own[k].astype(F32) + received[k].astype(F32)).astype(BF)

    return call(
        body, "pair", [VMEM, VMEM], tuple(out((edges, share, size), BF) for _ in range(chips))
    )


def pack_kernel(edges, slots, size, share, sectors, with_ids):
    height = CAP * share + EXTRA

    def body(meta, sums, first, second, third, fourth, message, seen):
        meta = Meta(meta, edges, slots)
        message[...] = jnp.zeros_like(message)
        line = lax.broadcasted_iota(jnp.int32, (EXTRA, size), 0)
        lane = lax.broadcasted_iota(jnp.int32, (EXTRA, size), 1)
        tail = sums[...]
        if with_ids:
            tail = jnp.where((line == ID_ROW) & (lane < CAP), -1.0, tail)
        for s in range(sectors):
            seen[s] = 0
            message[s, CAP * share :] = tail.astype(BF)
        for e in range(edges):
            owner = meta.edge(OWNER, e)
            rank = seen[owner]
            seen[owner] = rank + 1
            value = first[e].astype(F32) + second[e].astype(F32)
            value = value + (third[e].astype(F32) + fourth[e].astype(F32))
            message[owner, pl.ds(pl.multiple_of(rank * share, share), share)] = value.astype(BF)
            if with_ids:
                slot = meta.edge(SLOT, e).astype(F32)
                here = message[owner, CAP * share :].astype(F32)
                here = jnp.where((line == ID_ROW) & (lane == rank), slot, here)
                message[owner, CAP * share :] = here.astype(BF)

    return call(
        body,
        "pack",
        [SMEM] + [VMEM] * 5,
        out((sectors, height, size), BF),
        [pltpu.SMEM((sectors,), jnp.int32)],
    )


def image_kernel(k, edges, slots, size, share, sectors):
    def body(meta, arrived, vector, state, *refs):
        meta = Meta(meta, edges, slots)
        bases = refs[: k - 1]
        images = refs[k - 1 : 2 * k - 2]
        if k == 1:
            image, basis, message, new_state, ids, acc, slot_lanes, wide_ids = refs
            line = lax.broadcasted_iota(jnp.int32, (EXTRA, size), 0)
            for s in range(sectors):
                tail = arrived[s, CAP * share :].astype(F32)
                slot = jnp.sum(jnp.where(line == ID_ROW, tail, 0.0), axis=0, keepdims=True)
                slot = jnp.where(slot < 0.0, float(slots), slot)
                slot_lanes[s : s + 1] = slot.astype(jnp.int32)
            pltpu.sync_copy(slot_lanes, wide_ids)
            for s in range(sectors):
                for c in range(CAP):
                    ids[s * CAP + c] = wide_ids[s, c]
        else:
            ids, image, basis, message, new_state, acc = refs[2 * k - 2 :]
        sums = jnp.zeros((EXTRA, size), F32)
        acc[...] = jnp.zeros_like(acc)
        for s in range(sectors):
            sums = sums + arrived[s, CAP * share :].astype(F32)
            for c in range(CAP):
                slot = ids[s * CAP + c]
                acc[slot] = acc[slot] + arrived[s, c * share : (c + 1) * share].astype(F32)
        sums = jnp.sum(sums, axis=1, keepdims=True)
        total_of = [sums[j : j + 1] for j in range(k)]
        new_state[...] = state[...]

        def gram(i, j):
            row = 8 + 4 * max(i, j) + min(i, j)
            return state[row : row + 1, 0:1]

        def keep(row, value):
            new_state[row : row + 1] = jnp.broadcast_to(value, (1, size))

        project = total_of[: k - 1]
        length = total_of[k - 1]
        crossed = []
        for i in range(k - 1):
            mixed = jnp.zeros((1, 1), F32)
            for j in range(k - 1):
                mixed = mixed + gram(i, j) * project[j]
            crossed.append(mixed)
            length = length + project[i] * (mixed - 2.0 * project[i])
        length = jnp.maximum(length, 0.0)
        scale = 1.0 / jnp.sqrt(length + 1e-6)
        keep(4, scale)
        for j in range(k - 1):
            keep(5 + j, project[j])
            keep(8 + 4 * (k - 1) + j, scale * (project[j] - crossed[j]))
        keep(8 + 4 * (k - 1) + k - 1, length * scale * scale)
        first_row = meta.place() * share
        for b in range(slots):
            value = jnp.where(mask_of(meta, b, (share, size), first_row), acc[b], 0.0)
            direction = vector[b]
            for j in range(k - 1):
                value = value - project[j] * images[j][b]
                direction = direction - project[j] * bases[j][b]
            value = value * scale
            direction = direction * scale
            image[b] = value
            basis[b] = direction
            message[b] = value.astype(BF)

    rows = (slots, share, size)
    shapes = [out(rows, F32), out(rows, F32), out(rows, BF), out((24, size), F32)]
    specs = [VMEM] * 4
    scratch = [pltpu.VMEM((slots + 1, share, size), F32)]
    if k == 1:
        shapes.append(out((sectors * CAP,), jnp.int32))
        specs.append(SMEM)
        scratch.append(pltpu.VMEM((sectors, size), jnp.int32))
        scratch.append(pltpu.SMEM((sectors, size), jnp.int32))
    return call(
        body,
        "image",
        [SMEM] + [VMEM] * (3 + 2 * (k - 1)) + ([SMEM] if k > 1 else []),
        tuple(shapes),
        scratch,
        out_specs=tuple(specs),
    )


def gather_kernel(slots, size, share, chips):
    def body(*refs):
        for k in range(chips):
            refs[chips][k] = refs[k][...]

    return call(body, "gather", [VMEM] * chips, out((chips, slots, share, size), BF))


def weigh_kernel(k, edges, slots, size, share, sectors, chips):
    def body(meta, mine, other, vector, state, *refs):
        meta = Meta(meta, edges, slots)
        bases = refs[: k - 1]
        image, basis, message = refs[k - 1 :]
        x = meta.place() // 2
        c = lax.rem(meta.place(), 2)
        for j in range(chips):
            origin = 2 * lax.bitwise_xor(x, j)
            near = pl.multiple_of((origin + c) * share, share)
            far = pl.multiple_of((origin + 1 - c) * share, share)
            image[:, pl.ds(near, share)] = mine[j]
            image[:, pl.ds(far, share)] = other[j]
        scale = state[4:5]
        project = [state[5 + j : 6 + j] for j in range(k - 1)]

        def step(b, acc):
            direction = vector[b]
            for j in range(k - 1):
                direction = direction - project[j] * bases[j][b]
            direction = direction * scale
            basis[b] = direction
            return acc + fold(direction * image[b].astype(F32))

        acc = lax.fori_loop(0, slots, step, jnp.zeros((8, size), F32), unroll=2)
        message[...] = jnp.broadcast_to(total(acc)[None], (sectors, 1, size))

    return call(
        body,
        "weigh",
        [SMEM] + [VMEM] * (3 + k),
        (
            out((slots, size, size), BF),
            out((slots, size, size), F32),
            out((sectors, 1, size), F32),
        ),
    )


def correct_kernel(k, edges, slots, size, share, sectors, last):
    def body(meta, thetas, whole_image, whole_basis, shift, image, basis, state, *refs):
        meta = Meta(meta, edges, slots)
        bases = refs[: k - 1]
        if last:
            corrected, sums, new_state, stacked, sems = refs[2 * k - 2 :]
            sources = list(refs[k - 1 : 2 * k - 2]) + [image]
            copies = [
                pltpu.make_async_copy(source, stacked.at[j], sems.at[j])
                for j, source in enumerate(sources)
            ]
            for copy in copies:
                copy.start()
        else:
            whole, xin, corrected, sums, new_state = refs[k - 1 :]
        theta = jnp.sum(thetas[...].reshape(sectors, size), axis=0, keepdims=True)
        new_state[...] = state[...]
        new_state[k - 1 : k] = theta
        first_row = pl.multiple_of(meta.place() * share, share)

        def residual(mask, value, direction, moved):
            bottom = jnp.maximum(jnp.abs(moved - theta), 1.0)
            return jnp.where(mask, (value - theta * direction) / bottom, 0.0)

        def step(b, carry):
            direction = whole_basis[b]
            value = residual(
                mask_of(meta, b, (size, size), 0),
                whole_image[b].astype(F32),
                direction,
                shift[b],
            )
            if not last:
                whole[b] = value
                xin[b] = value.astype(BF)
            corrected[b] = residual(
                mask_of(meta, b, (share, size), first_row),
                image[b],
                basis[b],
                shift[b, pl.ds(first_row, share)],
            )
            others = [bases[j][b] for j in range(k - 1)] + [direction, value]
            return tuple(a + fold(value * o) for a, o in zip(carry, others))

        carry = lax.fori_loop(
            0, slots, step, tuple(jnp.zeros((8, size), F32) for _ in range(k + 1)), unroll=2
        )
        if last:
            line = lax.broadcasted_iota(jnp.int32, (EXTRA, size), 0)
            tail = jnp.zeros((EXTRA, size), F32)
            for j in range(k + 1):
                tail = jnp.where(line == j, total(carry[j]), tail)
            sums[...] = jnp.broadcast_to(tail[None], (sectors, EXTRA, size))
            for copy in copies:
                copy.wait()
        else:
            tail = jnp.zeros((EXTRA, size), F32)
            for j in range(k + 1):
                tail = tail + three_parts(total(carry[j]), j, EXTRA)
            sums[...] = tail

    blocks = out((slots, size, size), F32)
    shapes = [out((slots, share, size), F32), out((EXTRA, size), F32), out((24, size), F32)]
    if last:
        shapes[1] = out((sectors, EXTRA, size), F32)
        shapes.append(out((k, slots, share, size), F32))
        return call(
            body,
            "correct",
            [SMEM] + [VMEM] * (5 + 2 * k),
            tuple(shapes),
            [pltpu.SemaphoreType.DMA((k,))],
            out_specs=(VMEM, VMEM, VMEM, FAR),
        )
    shapes = [blocks, out((slots, size, size), BF)] + shapes
    return call(body, "correct", [SMEM] + [VMEM] * (6 + k), tuple(shapes))


def finish_kernel(slots, size, share, sectors):
    k = APPLIES

    def body(sums, vector, state, *refs):
        bases = refs[:k]
        final, ritz = refs[k:]
        added = jnp.sum(sums[...], axis=0)
        project = [added[j : j + 1] for j in range(k)]
        length = added[k : k + 1]
        for i in range(k):
            mixed = jnp.zeros((1, size), F32)
            for j in range(k):
                row = 8 + 4 * max(i, j) + min(i, j)
                mixed = mixed + state[row : row + 1] * project[j]
            length = length + project[i] * (mixed - 2.0 * project[i])
        scale = 1.0 / jnp.sqrt(jnp.maximum(length, 0.0) + 1e-6)
        for b in range(slots):
            value = vector[b]
            for j in range(k):
                value = value - project[j] * bases[j][b]
            final[b] = value * scale
        for j in range(k):
            ritz[j] = jnp.max(state[j : j + 1])

    return call(
        body,
        "finish",
        [VMEM] * (3 + k),
        (out((slots, share, size), F32), out((k,), F32)),
        out_specs=(VMEM, SMEM),
    )


def per_device(
    guess,
    diag_shift,
    block_rows,
    block_cols,
    left_env,
    right_env,
    edge_input,
    edge_left,
    edge_right,
    edge_owner,
    edge_slot,
):
    slots, size, _ = guess.shape
    sectors = lax.axis_size("sector")
    terms = lax.axis_size("mpo")
    edges = edge_input.shape[0]
    group = left_env.shape[0]
    share = size // terms
    chips = terms // 2
    place = lax.axis_index("mpo")
    core_swap = [(i, i ^ 1) for i in range(terms)]
    meta = jnp.concatenate(
        [
            edge_input,
            edge_left,
            edge_right,
            edge_owner[:, 0],
            edge_slot,
            block_rows,
            block_cols,
            place[None].astype(jnp.int32),
        ]
    )

    def over_sector(values):
        return lax.all_to_all(values, "sector", 0, 0, tiled=True)

    def chip_pair(values, k):
        pairs = [(i, 2 * ((i // 2) ^ k) + i % 2) for i in range(terms)]
        return lax.ppermute(values, "mpo", pairs)

    def chip_shift(values, k):
        pairs = [(i, (i + 2 * k) % terms) for i in range(terms)]
        return lax.ppermute(values, "mpo", pairs)

    def far(values):
        return pltpu.with_memory_space_constraint(values, pltpu.HBM)

    vector, xin, mine, sums, state, right_near, left_near, own, send = begin_kernel(
        edges, slots, size, share, group, chips
    )(meta, far(guess), far(right_env), far(left_env))
    bases, images, whole_bases, ids = [], [], [], []
    for k in range(1, APPLIES + 1):
        if k > 1:
            own, send, right_near, left_near = couple_kernel(
                edges, slots, size, share, group, chips
            )(meta, xin, right_near, left_near)
        received = lax.ppermute(send, "mpo", core_swap)
        parts = pair_kernel(edges, size, share, chips)(own, received)
        shifted = [parts[0]] + [chip_shift(parts[j], j) for j in range(1, chips)]
        message = pack_kernel(edges, slots, size, share, sectors, k == 1)(meta, sums, *shifted)
        arrived = over_sector(message)
        result = image_kernel(k, edges, slots, size, share, sectors)(
            meta, arrived, mine, state, *bases, *images, *ids
        )
        image, basis, outgoing, state = result[:4]
        if k == 1:
            ids = result[4:]
        rows = [outgoing] + [chip_pair(outgoing, j) for j in range(1, chips)]
        near_rows = gather_kernel(slots, size, share, chips)(*rows)
        far_rows = lax.ppermute(near_rows, "mpo", core_swap)
        whole_image, whole_basis, parts = weigh_kernel(
            k, edges, slots, size, share, sectors, chips
        )(
            meta, near_rows, far_rows, vector, state, *whole_bases
        )
        thetas = over_sector(parts)
        last = k == APPLIES
        others = [*whole_bases, *images] if last else whole_bases
        result = correct_kernel(k, edges, slots, size, share, sectors, last)(
            meta, thetas, whole_image, whole_basis, diag_shift, image, basis, state, *others
        )
        if last:
            mine, sums, state, stacked = result
        else:
            vector, xin, mine, sums, state = result
            whole_bases.append(whole_basis)
        bases.append(basis)
        images.append(image)
    final, ritz = finish_kernel(slots, size, share, sectors)(
        over_sector(sums), mine, state, *bases
    )
    return stacked, final, ritz


def solution(mesh):
    return jax.shard_map(
        per_device,
        mesh=mesh,
        in_specs=(
            P("sector", None, None),
            P("sector", None, None),
            P("sector"),
            P("sector"),
            P("mpo", "sector", None, None),
            P("mpo", "sector", None, None),
            P("sector"),
            P("sector"),
            P("sector"),
            P("sector", None),
            P("sector"),
        ),
        out_specs=(P(None, "sector", "mpo", None), P("sector", "mpo", None), P()),
        check_vma=False,
    )
```

```python
import jax
import jax.numpy as jnp
from jax import lax
from jax.experimental import pallas as pl
from jax.experimental.pallas import tpu as pltpu
from jax.sharding import PartitionSpec as P

APPLIES = 3
CAP = 2
EXTRA = 8
ID_ROW = 4
UNROLL = 16
BF = jnp.bfloat16
F32 = jnp.float32
VMEM = pl.BlockSpec(memory_space=pltpu.VMEM)
SMEM = pl.BlockSpec(memory_space=pltpu.SMEM)
FAR = pl.BlockSpec(memory_space=pltpu.HBM)
PIECES = 4


class Meta:
    def __init__(self, ref, edges, slots):
        self.ref, self.edges, self.slots = ref, edges, slots

    def edge(self, column, e):
        return self.ref[column * self.edges + e]

    def rows(self, b):
        return self.ref[5 * self.edges + b]

    def cols(self, b):
        return self.ref[5 * self.edges + self.slots + b]

    def place(self):
        return self.ref[5 * self.edges + 2 * self.slots]


IN, LEFT, RIGHT, OWNER, SLOT = range(5)


def call(body, name, in_specs, out_shape, scratch=(), mib=8, aliases={}, out_specs=None):
    return pl.pallas_call(
        body,
        name=name,
        in_specs=in_specs,
        out_shape=out_shape,
        out_specs=out_specs or jax.tree.map(lambda _: VMEM, out_shape),
        input_output_aliases=aliases,
        scratch_shapes=scratch,
        compiler_params=pltpu.CompilerParams(vmem_limit_bytes=mib << 20),
    )


def out(shape, dtype):
    return jax.ShapeDtypeStruct(shape, dtype)


def total(values):
    return jnp.sum(jnp.sum(values, axis=0, keepdims=True), axis=1, keepdims=True)


def fold(values):
    return jnp.sum(values.reshape(-1, 8, values.shape[-1]), axis=0)


def three_parts(value, row, height):
    high = value.astype(BF).astype(F32)
    middle = (value - high).astype(BF).astype(F32)
    low = value - high - middle
    lane = lax.broadcasted_iota(jnp.int32, (height, 128), 1)
    line = lax.broadcasted_iota(jnp.int32, (height, 128), 0)
    spread = jnp.where(lane == 0, high, jnp.where(lane == 1, middle, jnp.where(lane == 2, low, 0.0)))
    return jnp.where(line == row, spread, 0.0)


def mask_of(meta, block, shape, first_row):
    line = lax.broadcasted_iota(jnp.int32, shape, 0) + first_row
    lane = lax.broadcasted_iota(jnp.int32, shape, 1)
    return (line < meta.rows(block)) & (lane < meta.cols(block))


def couple_rows(meta, chips, share, own, send, tmp, e, u, value):
    x = meta.place() // 2
    c = lax.rem(meta.place(), 2)
    tmp[u] = value.astype(BF)
    for k in range(chips):
        to = lax.rem(x + k, chips)
        mine = pl.multiple_of((2 * to + c) * share, share)
        other = pl.multiple_of((2 * to + 1 - c) * share, share)
        own[k, e] = tmp[u, pl.ds(mine, share)]
        send[k, e] = tmp[u, pl.ds(other, share)]


def add_terms(meta, xin, right, left, e, terms, acc):
    value = xin[meta.edge(IN, e)]
    le = meta.edge(LEFT, e)
    re = meta.edge(RIGHT, e)
    for w in terms:
        half = jnp.dot(value, right[w, re], preferred_element_type=F32).astype(BF)
        term = jnp.dot(left[w, le], half, preferred_element_type=F32)
        acc = term if acc is None else acc + term
    return acc


def unrolled(edges, one):
    def step(t, carry):
        for u in range(UNROLL):
            one(t * UNROLL + u, u)
        return carry

    lax.fori_loop(0, edges // UNROLL, step, 0)


def start_kernel(edges, slots, size, share, group):
    terms = group // PIECES

    def body(meta, far_guess, right, left, *refs):
        meta = Meta(meta, edges, slots)
        vector, xin, mine, sums, state, right_near, left_near, guess, sems, guess_sem = refs
        first = pltpu.make_async_copy(far_guess, guess, guess_sem)
        first.start()
        copies = []
        for i, (far, near) in enumerate(((right, right_near), (left, left_near))):
            for p in range(PIECES):
                part = pl.ds(p * terms, terms)
                copies.append(pltpu.make_async_copy(far.at[part], near.at[part], sems.at[i, p]))
        for copy in copies:
            copy.start()
        state[...] = jnp.zeros_like(state)
        first_row = pl.multiple_of(meta.place() * share, share)
        first.wait()

        def block(b, squares):
            value = jnp.where(mask_of(meta, b, (size, size), 0), guess[b], 0.0)
            vector[b] = value
            xin[b] = value.astype(BF)
            rows = guess[b, pl.ds(first_row, share)]
            mine[b] = jnp.where(mask_of(meta, b, (share, size), first_row), rows, 0.0)
            return squares + fold(value * value)

        squares = lax.fori_loop(0, slots, block, jnp.zeros((8, size), F32), unroll=4)
        sums[...] = three_parts(total(squares), 0, EXTRA)
        for copy in copies:
            copy.wait()

    near = pltpu.VMEM((group, slots, size, size), BF)
    return call(
        body,
        "start",
        [SMEM, FAR, FAR, FAR],
        (
            out((slots, size, size), F32),
            out((slots, size, size), BF),
            out((slots, share, size), F32),
            out((EXTRA, size), F32),
            out((24, size), F32),
            near,
            near,
        ),
        [
            pltpu.VMEM((slots, size, size), F32),
            pltpu.SemaphoreType.DMA((2, PIECES)),
            pltpu.SemaphoreType.DMA,
        ],
    )


def couple_kernel(edges, slots, size, share, group, chips):
    def body(meta, xin, right, left, own, send, *refs):
        meta = Meta(meta, edges, slots)
        tmp = refs[-1]

        def one(e, u):
            value = add_terms(meta, xin, right, left, e, range(group), None)
            couple_rows(meta, chips, share, own, send, tmp, e, u, value)

        unrolled(edges, one)

    shape = out((chips, edges, share, size), BF)
    near = pltpu.VMEM((group, slots, size, size), BF)
    return call(
        body,
        "couple",
        [SMEM, VMEM, VMEM, VMEM],
        (shape, shape, near, near),
        [pltpu.VMEM((UNROLL, size, size), BF)],
        aliases={2: 2, 3: 3},
    )


def pair_kernel(edges, size, share, chips):
    def body(own, received, *parts):
        for k in range(chips):
            parts[k][...] = (own[k].astype(F32) + received[k].astype(F32)).astype(BF)

    return call(
        body, "pair", [VMEM, VMEM], tuple(out((edges, share, size), BF) for _ in range(chips))
    )


def pack_kernel(edges, slots, size, share, sectors, with_ids):
    height = CAP * share + EXTRA

    def body(meta, sums, first, second, third, fourth, message, seen):
        meta = Meta(meta, edges, slots)
        message[...] = jnp.zeros_like(message)
        line = lax.broadcasted_iota(jnp.int32, (EXTRA, size), 0)
        lane = lax.broadcasted_iota(jnp.int32, (EXTRA, size), 1)
        tail = sums[...]
        if with_ids:
            tail = jnp.where((line == ID_ROW) & (lane < CAP), -1.0, tail)
        for s in range(sectors):
            seen[s] = 0
            message[s, CAP * share :] = tail.astype(BF)
        for e in range(edges):
            owner = meta.edge(OWNER, e)
            rank = seen[owner]
            seen[owner] = rank + 1
            value = first[e].astype(F32) + second[e].astype(F32)
            value = value + (third[e].astype(F32) + fourth[e].astype(F32))
            message[owner, pl.ds(pl.multiple_of(rank * share, share), share)] = value.astype(BF)
            if with_ids:
                slot = meta.edge(SLOT, e).astype(F32)
                here = message[owner, CAP * share :].astype(F32)
                here = jnp.where((line == ID_ROW) & (lane == rank), slot, here)
                message[owner, CAP * share :] = here.astype(BF)

    return call(
        body,
        "pack",
        [SMEM] + [VMEM] * 5,
        out((sectors, height, size), BF),
        [pltpu.SMEM((sectors,), jnp.int32)],
    )


def image_kernel(k, edges, slots, size, share, sectors):
    def body(meta, arrived, vector, state, *refs):
        meta = Meta(meta, edges, slots)
        bases = refs[: k - 1]
        images = refs[k - 1 : 2 * k - 2]
        if k == 1:
            image, basis, message, new_state, ids, acc, slot_lanes, wide_ids = refs
            for s in range(sectors):
                tail = arrived[s, CAP * share :].astype(F32)
                slot = tail[ID_ROW : ID_ROW + 1]
                slot = jnp.where(slot < 0.0, float(slots), slot)
                slot_lanes[s : s + 1] = slot.astype(jnp.int32)
            pltpu.sync_copy(slot_lanes, wide_ids)
            for s in range(sectors):
                for c in range(CAP):
                    ids[s * CAP + c] = wide_ids[s, c]
        else:
            ids, image, basis, message, new_state, acc = refs[2 * k - 2 :]
        sums = jnp.zeros((EXTRA, size), F32)
        acc[...] = jnp.zeros_like(acc)
        for s in range(sectors):
            sums = sums + arrived[s, CAP * share :].astype(F32)
            for c in range(CAP):
                slot = ids[s * CAP + c]
                acc[slot] = acc[slot] + arrived[s, c * share : (c + 1) * share].astype(F32)
        sums = jnp.sum(sums, axis=1, keepdims=True)
        total_of = [sums[j : j + 1] for j in range(k)]
        new_state[...] = state[...]

        def gram(i, j):
            row = 8 + 4 * max(i, j) + min(i, j)
            return state[row : row + 1, 0:1]

        def keep(row, value):
            new_state[row : row + 1] = jnp.broadcast_to(value, (1, size))

        project = total_of[: k - 1]
        length = total_of[k - 1]
        crossed = []
        for i in range(k - 1):
            mixed = jnp.zeros((1, 1), F32)
            for j in range(k - 1):
                mixed = mixed + gram(i, j) * project[j]
            crossed.append(mixed)
            length = length + project[i] * (mixed - 2.0 * project[i])
        length = jnp.maximum(length, 0.0)
        scale = 1.0 / jnp.sqrt(length + 1e-6)
        keep(4, scale)
        for j in range(k - 1):
            keep(5 + j, project[j])
            keep(8 + 4 * (k - 1) + j, scale * (project[j] - crossed[j]))
        keep(8 + 4 * (k - 1) + k - 1, length * scale * scale)
        first_row = meta.place() * share
        for b in range(slots):
            value = jnp.where(mask_of(meta, b, (share, size), first_row), acc[b], 0.0)
            direction = vector[b]
            for j in range(k - 1):
                value = value - project[j] * images[j][b]
                direction = direction - project[j] * bases[j][b]
            value = value * scale
            direction = direction * scale
            image[b] = value
            basis[b] = direction
            message[b] = value.astype(BF)

    rows = (slots, share, size)
    shapes = [out(rows, F32), out(rows, F32), out(rows, BF), out((24, size), F32)]
    specs = [VMEM] * 4
    scratch = [pltpu.VMEM((slots + 1, share, size), F32)]
    if k == 1:
        shapes.append(out((sectors * CAP,), jnp.int32))
        specs.append(SMEM)
        scratch.append(pltpu.VMEM((sectors, size), jnp.int32))
        scratch.append(pltpu.SMEM((sectors, size), jnp.int32))
    return call(
        body,
        "image",
        [SMEM] + [VMEM] * (3 + 2 * (k - 1)) + ([SMEM] if k > 1 else []),
        tuple(shapes),
        scratch,
        out_specs=tuple(specs),
    )


def gather_kernel(slots, size, share, chips):
    def body(*refs):
        for k in range(chips):
            refs[chips][k] = refs[k][...]

    return call(body, "gather", [VMEM] * chips, out((chips, slots, share, size), BF))


def weigh_kernel(k, edges, slots, size, share, sectors, chips):
    def body(meta, mine, other, vector, state, *refs):
        meta = Meta(meta, edges, slots)
        bases = refs[: k - 1]
        image, basis, message = refs[k - 1 :]
        x = meta.place() // 2
        c = lax.rem(meta.place(), 2)
        for j in range(chips):
            origin = 2 * lax.bitwise_xor(x, j)
            near = pl.multiple_of((origin + c) * share, share)
            far = pl.multiple_of((origin + 1 - c) * share, share)
            image[:, pl.ds(near, share)] = mine[j]
            image[:, pl.ds(far, share)] = other[j]
        scale = state[4:5]
        project = [state[5 + j : 6 + j] for j in range(k - 1)]

        def step(b, acc):
            direction = vector[b]
            for j in range(k - 1):
                direction = direction - project[j] * bases[j][b]
            direction = direction * scale
            basis[b] = direction
            return acc + fold(direction * image[b].astype(F32))

        acc = lax.fori_loop(0, slots, step, jnp.zeros((8, size), F32), unroll=2)
        message[...] = jnp.broadcast_to(total(acc)[None], (sectors, 1, size))

    return call(
        body,
        "weigh",
        [SMEM] + [VMEM] * (3 + k),
        (
            out((slots, size, size), BF),
            out((slots, size, size), F32),
            out((sectors, 1, size), F32),
        ),
    )


def correct_kernel(k, edges, slots, size, share, sectors, last):
    def body(meta, thetas, whole_image, whole_basis, shift, image, basis, state, *refs):
        meta = Meta(meta, edges, slots)
        bases = refs[: k - 1]
        if last:
            corrected, sums, new_state, stacked, sems = refs[2 * k - 2 :]
            sources = list(refs[k - 1 : 2 * k - 2]) + [image]
            copies = [
                pltpu.make_async_copy(source, stacked.at[j], sems.at[j])
                for j, source in enumerate(sources)
            ]
            for copy in copies:
                copy.start()
        else:
            whole, xin, corrected, sums, new_state = refs[k - 1 :]
        theta = jnp.sum(thetas[...].reshape(sectors, size), axis=0, keepdims=True)
        new_state[...] = state[...]
        new_state[k - 1 : k] = theta
        first_row = pl.multiple_of(meta.place() * share, share)

        def residual(mask, value, direction, moved):
            bottom = jnp.maximum(jnp.abs(moved - theta), 1.0)
            return jnp.where(mask, (value - theta * direction) / bottom, 0.0)

        def step(b, carry):
            direction = whole_basis[b]
            value = residual(
                mask_of(meta, b, (size, size), 0),
                whole_image[b].astype(F32),
                direction,
                shift[b],
            )
            if not last:
                whole[b] = value
                xin[b] = value.astype(BF)
            corrected[b] = residual(
                mask_of(meta, b, (share, size), first_row),
                image[b],
                basis[b],
                shift[b, pl.ds(first_row, share)],
            )
            others = [bases[j][b] for j in range(k - 1)] + [direction, value]
            return tuple(a + fold(value * o) for a, o in zip(carry, others))

        carry = lax.fori_loop(
            0, slots, step, tuple(jnp.zeros((8, size), F32) for _ in range(k + 1)), unroll=2
        )
        if last:
            line = lax.broadcasted_iota(jnp.int32, (EXTRA, size), 0)
            tail = jnp.zeros((EXTRA, size), F32)
            for j in range(k + 1):
                tail = jnp.where(line == j, total(carry[j]), tail)
            sums[...] = jnp.broadcast_to(tail[None], (sectors, EXTRA, size))
            for copy in copies:
                copy.wait()
        else:
            tail = jnp.zeros((EXTRA, size), F32)
            for j in range(k + 1):
                tail = tail + three_parts(total(carry[j]), j, EXTRA)
            sums[...] = tail

    blocks = out((slots, size, size), F32)
    shapes = [out((slots, share, size), F32), out((EXTRA, size), F32), out((24, size), F32)]
    if last:
        shapes[1] = out((sectors, EXTRA, size), F32)
        shapes.append(out((k, slots, share, size), F32))
        return call(
            body,
            "correct",
            [SMEM] + [VMEM] * (5 + 2 * k),
            tuple(shapes),
            [pltpu.SemaphoreType.DMA((k,))],
            out_specs=(VMEM, VMEM, VMEM, FAR),
        )
    shapes = [blocks, out((slots, size, size), BF)] + shapes
    return call(body, "correct", [SMEM] + [VMEM] * (6 + k), tuple(shapes))


def finish_kernel(slots, size, share, sectors):
    k = APPLIES

    def body(sums, vector, state, *refs):
        bases = refs[:k]
        final, ritz = refs[k:]
        added = jnp.sum(sums[...], axis=0)
        project = [added[j : j + 1] for j in range(k)]
        length = added[k : k + 1]
        for i in range(k):
            mixed = jnp.zeros((1, size), F32)
            for j in range(k):
                row = 8 + 4 * max(i, j) + min(i, j)
                mixed = mixed + state[row : row + 1] * project[j]
            length = length + project[i] * (mixed - 2.0 * project[i])
        scale = 1.0 / jnp.sqrt(jnp.maximum(length, 0.0) + 1e-6)
        for b in range(slots):
            value = vector[b]
            for j in range(k):
                value = value - project[j] * bases[j][b]
            final[b] = value * scale
        for j in range(k):
            ritz[j] = jnp.max(state[j : j + 1])

    return call(
        body,
        "finish",
        [VMEM] * (3 + k),
        (out((slots, share, size), F32), out((k,), F32)),
        out_specs=(VMEM, SMEM),
    )


def per_device(
    guess,
    diag_shift,
    block_rows,
    block_cols,
    left_env,
    right_env,
    edge_input,
    edge_left,
    edge_right,
    edge_owner,
    edge_slot,
):
    slots, size, _ = guess.shape
    sectors = lax.axis_size("sector")
    terms = lax.axis_size("mpo")
    edges = edge_input.shape[0]
    group = left_env.shape[0]
    share = size // terms
    chips = terms // 2
    place = lax.axis_index("mpo")
    core_swap = [(i, i ^ 1) for i in range(terms)]
    meta = jnp.concatenate(
        [
            edge_input,
            edge_left,
            edge_right,
            edge_owner[:, 0],
            edge_slot,
            block_rows,
            block_cols,
            place[None].astype(jnp.int32),
        ]
    )

    def over_sector(values):
        return lax.all_to_all(values, "sector", 0, 0, tiled=True)

    def chip_pair(values, k):
        pairs = [(i, 2 * ((i // 2) ^ k) + i % 2) for i in range(terms)]
        return lax.ppermute(values, "mpo", pairs)

    def chip_shift(values, k):
        pairs = [(i, (i + 2 * k) % terms) for i in range(terms)]
        return lax.ppermute(values, "mpo", pairs)

    def far(values):
        return pltpu.with_memory_space_constraint(values, pltpu.HBM)

    vector, xin, mine, sums, state, right_near, left_near = start_kernel(
        edges, slots, size, share, group
    )(meta, far(guess), far(right_env), far(left_env))
    bases, images, whole_bases, ids = [], [], [], []
    for k in range(1, APPLIES + 1):
        own, send, right_near, left_near = couple_kernel(edges, slots, size, share, group, chips)(
            meta, xin, right_near, left_near
        )
        received = lax.ppermute(send, "mpo", core_swap)
        parts = pair_kernel(edges, size, share, chips)(own, received)
        shifted = [parts[0]] + [chip_shift(parts[j], j) for j in range(1, chips)]
        message = pack_kernel(edges, slots, size, share, sectors, k == 1)(meta, sums, *shifted)
        arrived = over_sector(message)
        result = image_kernel(k, edges, slots, size, share, sectors)(
            meta, arrived, mine, state, *bases, *images, *ids
        )
        image, basis, outgoing, state = result[:4]
        if k == 1:
            ids = result[4:]
        rows = [outgoing] + [chip_pair(outgoing, j) for j in range(1, chips)]
        near_rows = gather_kernel(slots, size, share, chips)(*rows)
        far_rows = lax.ppermute(near_rows, "mpo", core_swap)
        whole_image, whole_basis, parts = weigh_kernel(
            k, edges, slots, size, share, sectors, chips
        )(
            meta, near_rows, far_rows, vector, state, *whole_bases
        )
        thetas = over_sector(parts)
        last = k == APPLIES
        others = [*whole_bases, *images] if last else whole_bases
        result = correct_kernel(k, edges, slots, size, share, sectors, last)(
            meta, thetas, whole_image, whole_basis, diag_shift, image, basis, state, *others
        )
        if last:
            mine, sums, state, stacked = result
        else:
            vector, xin, mine, sums, state = result
            whole_bases.append(whole_basis)
        bases.append(basis)
        images.append(image)
    final, ritz = finish_kernel(slots, size, share, sectors)(
        over_sector(sums), mine, state, *bases
    )
    return stacked, final, ritz


def solution(mesh):
    return jax.shard_map(
        per_device,
        mesh=mesh,
        in_specs=(
            P("sector", None, None),
            P("sector", None, None),
            P("sector"),
            P("sector"),
            P("mpo", "sector", None, None),
            P("mpo", "sector", None, None),
            P("sector"),
            P("sector"),
            P("sector"),
            P("sector", None),
            P("sector"),
        ),
        out_specs=(P(None, "sector", "mpo", None), P("sector", "mpo", None), P()),
        check_vma=False,
    )
```

```python
import jax
import jax.numpy as jnp
from jax import lax
from jax.experimental import pallas as pl
from jax.experimental.pallas import tpu as pltpu
from jax.sharding import PartitionSpec as P

APPLIES = 3
CAP = 2
EXTRA = 8
ID_ROW = 4
UNROLL = 16
BF = jnp.bfloat16
F32 = jnp.float32
VMEM = pl.BlockSpec(memory_space=pltpu.VMEM)
SMEM = pl.BlockSpec(memory_space=pltpu.SMEM)
FAR = pl.BlockSpec(memory_space=pltpu.HBM)
PIECES = 4


class Meta:
    def __init__(self, ref, edges, slots):
        self.ref, self.edges, self.slots = ref, edges, slots

    def edge(self, column, e):
        return self.ref[column * self.edges + e]

    def rows(self, b):
        return self.ref[5 * self.edges + b]

    def cols(self, b):
        return self.ref[5 * self.edges + self.slots + b]

    def place(self):
        return self.ref[5 * self.edges + 2 * self.slots]


IN, LEFT, RIGHT, OWNER, SLOT = range(5)


def call(body, name, in_specs, out_shape, scratch=(), mib=8, aliases={}, out_specs=None):
    return pl.pallas_call(
        body,
        name=name,
        in_specs=in_specs,
        out_shape=out_shape,
        out_specs=out_specs or jax.tree.map(lambda _: VMEM, out_shape),
        input_output_aliases=aliases,
        scratch_shapes=scratch,
        compiler_params=pltpu.CompilerParams(vmem_limit_bytes=mib << 20),
    )


def out(shape, dtype):
    return jax.ShapeDtypeStruct(shape, dtype)


def total(values):
    return jnp.sum(jnp.sum(values, axis=0, keepdims=True), axis=1, keepdims=True)


def fold(values):
    return jnp.sum(values.reshape(-1, 8, values.shape[-1]), axis=0)


def three_parts(value, row, height):
    high = value.astype(BF).astype(F32)
    middle = (value - high).astype(BF).astype(F32)
    low = value - high - middle
    lane = lax.broadcasted_iota(jnp.int32, (height, 128), 1)
    line = lax.broadcasted_iota(jnp.int32, (height, 128), 0)
    spread = jnp.where(lane == 0, high, jnp.where(lane == 1, middle, jnp.where(lane == 2, low, 0.0)))
    return jnp.where(line == row, spread, 0.0)


def mask_of(meta, block, shape, first_row):
    line = lax.broadcasted_iota(jnp.int32, shape, 0) + first_row
    lane = lax.broadcasted_iota(jnp.int32, shape, 1)
    return (line < meta.rows(block)) & (lane < meta.cols(block))


def couple_rows(meta, chips, share, own, send, tmp, e, u, value):
    x = meta.place() // 2
    c = lax.rem(meta.place(), 2)
    tmp[u] = value.astype(BF)
    for k in range(chips):
        to = lax.rem(x + k, chips)
        mine = pl.multiple_of((2 * to + c) * share, share)
        other = pl.multiple_of((2 * to + 1 - c) * share, share)
        own[k, e] = tmp[u, pl.ds(mine, share)]
        send[k, e] = tmp[u, pl.ds(other, share)]


def add_terms(meta, xin, right, left, e, terms, acc):
    value = xin[meta.edge(IN, e)]
    le = meta.edge(LEFT, e)
    re = meta.edge(RIGHT, e)
    for w in terms:
        half = jnp.dot(value, right[w, re], preferred_element_type=F32).astype(BF)
        term = jnp.dot(left[w, le], half, preferred_element_type=F32)
        acc = term if acc is None else acc + term
    return acc


def unrolled(edges, one):
    def step(t, carry):
        for u in range(UNROLL):
            one(t * UNROLL + u, u)
        return carry

    lax.fori_loop(0, edges // UNROLL, step, 0)


def start_kernel(edges, slots, size, share, group):
    terms = group // PIECES

    def body(meta, far_guess, right, left, *refs):
        meta = Meta(meta, edges, slots)
        vector, xin, mine, sums, state, right_near, left_near, guess, sems, guess_sem = refs
        first = pltpu.make_async_copy(far_guess, guess, guess_sem)
        first.start()
        copies = []
        for i, (far, near) in enumerate(((right, right_near), (left, left_near))):
            for p in range(PIECES):
                part = pl.ds(p * terms, terms)
                copies.append(pltpu.make_async_copy(far.at[part], near.at[part], sems.at[i, p]))
        for copy in copies:
            copy.start()
        state[...] = jnp.zeros_like(state)
        first_row = pl.multiple_of(meta.place() * share, share)
        first.wait()

        def block(b, squares):
            value = jnp.where(mask_of(meta, b, (size, size), 0), guess[b], 0.0)
            vector[b] = value
            xin[b] = value.astype(BF)
            rows = guess[b, pl.ds(first_row, share)]
            mine[b] = jnp.where(mask_of(meta, b, (share, size), first_row), rows, 0.0)
            return squares + fold(value * value)

        squares = lax.fori_loop(0, slots, block, jnp.zeros((8, size), F32), unroll=4)
        sums[...] = three_parts(total(squares), 0, EXTRA)
        for copy in copies:
            copy.wait()

    near = pltpu.VMEM((group, slots, size, size), BF)
    return call(
        body,
        "start",
        [SMEM, FAR, FAR, FAR],
        (
            out((slots, size, size), F32),
            out((slots, size, size), BF),
            out((slots, share, size), F32),
            out((EXTRA, size), F32),
            out((24, size), F32),
            near,
            near,
        ),
        [
            pltpu.VMEM((slots, size, size), F32),
            pltpu.SemaphoreType.DMA((2, PIECES)),
            pltpu.SemaphoreType.DMA,
        ],
    )


def couple_kernel(edges, slots, size, share, group, chips):
    def body(meta, xin, right, left, own, send, *refs):
        meta = Meta(meta, edges, slots)
        tmp = refs[-1]

        def one(e, u):
            value = add_terms(meta, xin, right, left, e, range(group), None)
            couple_rows(meta, chips, share, own, send, tmp, e, u, value)

        unrolled(edges, one)

    shape = out((chips, edges, share, size), BF)
    near = pltpu.VMEM((group, slots, size, size), BF)
    return call(
        body,
        "couple",
        [SMEM, VMEM, VMEM, VMEM],
        (shape, shape, near, near),
        [pltpu.VMEM((UNROLL, size, size), BF)],
        aliases={2: 2, 3: 3},
    )


def pair_kernel(edges, size, share, chips):
    def body(own, received, *parts):
        for k in range(chips):
            parts[k][...] = (own[k].astype(F32) + received[k].astype(F32)).astype(BF)

    return call(
        body, "pair", [VMEM, VMEM], tuple(out((edges, share, size), BF) for _ in range(chips))
    )


def pack_kernel(edges, slots, size, share, sectors, with_ids):
    height = CAP * share + EXTRA

    def body(meta, sums, first, second, third, fourth, message, seen):
        meta = Meta(meta, edges, slots)
        message[...] = jnp.zeros_like(message)
        line = lax.broadcasted_iota(jnp.int32, (EXTRA, size), 0)
        lane = lax.broadcasted_iota(jnp.int32, (EXTRA, size), 1)
        tail = sums[...]
        if with_ids:
            tail = jnp.where((line == ID_ROW) & (lane < CAP), -1.0, tail)
        for s in range(sectors):
            seen[s] = 0
            message[s, CAP * share :] = tail.astype(BF)
        for e in range(edges):
            owner = meta.edge(OWNER, e)
            rank = seen[owner]
            seen[owner] = rank + 1
            value = first[e].astype(F32) + second[e].astype(F32)
            value = value + (third[e].astype(F32) + fourth[e].astype(F32))
            message[owner, pl.ds(pl.multiple_of(rank * share, share), share)] = value.astype(BF)
            if with_ids:
                slot = meta.edge(SLOT, e).astype(F32)
                here = message[owner, CAP * share :].astype(F32)
                here = jnp.where((line == ID_ROW) & (lane == rank), slot, here)
                message[owner, CAP * share :] = here.astype(BF)

    return call(
        body,
        "pack",
        [SMEM] + [VMEM] * 5,
        out((sectors, height, size), BF),
        [pltpu.SMEM((sectors,), jnp.int32)],
    )


def image_kernel(k, edges, slots, size, share, sectors):
    def body(meta, arrived, vector, state, *refs):
        meta = Meta(meta, edges, slots)
        bases = refs[: k - 1]
        images = refs[k - 1 : 2 * k - 2]
        if k == 1:
            image, basis, message, new_state, ids, acc, slot_lanes, wide_ids = refs
            for s in range(sectors):
                tail = arrived[s, CAP * share :].astype(F32)
                slot = tail[ID_ROW : ID_ROW + 1]
                slot = jnp.where(slot < 0.0, float(slots), slot)
                slot_lanes[s : s + 1] = slot.astype(jnp.int32)
            pltpu.sync_copy(slot_lanes, wide_ids)
            for s in range(sectors):
                for c in range(CAP):
                    ids[s * CAP + c] = wide_ids[s, c]
        else:
            ids, image, basis, message, new_state, acc = refs[2 * k - 2 :]
        sums = jnp.zeros((EXTRA, size), F32)
        acc[...] = jnp.zeros_like(acc)
        for s in range(sectors):
            sums = sums + arrived[s, CAP * share :].astype(F32)
            for c in range(CAP):
                slot = ids[s * CAP + c]
                acc[slot] = acc[slot] + arrived[s, c * share : (c + 1) * share].astype(F32)
        sums = jnp.sum(sums, axis=1, keepdims=True)
        total_of = [sums[j : j + 1] for j in range(k)]
        new_state[...] = state[...]

        def gram(i, j):
            row = 8 + 4 * max(i, j) + min(i, j)
            return state[row : row + 1, 0:1]

        def keep(row, value):
            new_state[row : row + 1] = jnp.broadcast_to(value, (1, size))

        project = total_of[: k - 1]
        length = total_of[k - 1]
        crossed = []
        for i in range(k - 1):
            mixed = jnp.zeros((1, 1), F32)
            for j in range(k - 1):
                mixed = mixed + gram(i, j) * project[j]
            crossed.append(mixed)
            length = length + project[i] * (mixed - 2.0 * project[i])
        length = jnp.maximum(length, 0.0)
        scale = 1.0 / jnp.sqrt(length + 1e-6)
        keep(4, scale)
        for j in range(k - 1):
            keep(5 + j, project[j])
            keep(8 + 4 * (k - 1) + j, scale * (project[j] - crossed[j]))
        keep(8 + 4 * (k - 1) + k - 1, length * scale * scale)
        first_row = meta.place() * share
        for b in range(slots):
            value = jnp.where(mask_of(meta, b, (share, size), first_row), acc[b], 0.0)
            direction = vector[b]
            for j in range(k - 1):
                value = value - project[j] * images[j][b]
                direction = direction - project[j] * bases[j][b]
            value = value * scale
            direction = direction * scale
            image[b] = value
            basis[b] = direction
            message[b] = value.astype(BF)

    rows = (slots, share, size)
    shapes = [out(rows, F32), out(rows, F32), out(rows, BF), out((24, size), F32)]
    specs = [VMEM] * 4
    scratch = [pltpu.VMEM((slots + 1, share, size), F32)]
    if k == 1:
        shapes.append(out((sectors * CAP,), jnp.int32))
        specs.append(SMEM)
        scratch.append(pltpu.VMEM((sectors, size), jnp.int32))
        scratch.append(pltpu.SMEM((sectors, size), jnp.int32))
    return call(
        body,
        "image",
        [SMEM] + [VMEM] * (3 + 2 * (k - 1)) + ([SMEM] if k > 1 else []),
        tuple(shapes),
        scratch,
        out_specs=tuple(specs),
    )


def gather_kernel(slots, size, share, chips):
    def body(*refs):
        for k in range(chips):
            refs[chips][k] = refs[k][...]

    return call(body, "gather", [VMEM] * chips, out((chips, slots, share, size), BF))


def weigh_kernel(k, edges, slots, size, share, sectors, chips):
    def body(meta, mine, other, vector, state, *refs):
        meta = Meta(meta, edges, slots)
        bases = refs[: k - 1]
        image, basis, message = refs[k - 1 :]
        x = meta.place() // 2
        c = lax.rem(meta.place(), 2)
        for j in range(chips):
            origin = 2 * lax.bitwise_xor(x, j)
            near = pl.multiple_of((origin + c) * share, share)
            far = pl.multiple_of((origin + 1 - c) * share, share)
            image[:, pl.ds(near, share)] = mine[j]
            image[:, pl.ds(far, share)] = other[j]
        scale = state[4:5]
        project = [state[5 + j : 6 + j] for j in range(k - 1)]

        def step(b, acc):
            direction = vector[b]
            for j in range(k - 1):
                direction = direction - project[j] * bases[j][b]
            direction = direction * scale
            basis[b] = direction
            return acc + fold(direction * image[b].astype(F32))

        acc = lax.fori_loop(0, slots, step, jnp.zeros((8, size), F32), unroll=4)
        message[...] = jnp.broadcast_to(total(acc)[None], (sectors, 1, size))

    return call(
        body,
        "weigh",
        [SMEM] + [VMEM] * (3 + k),
        (
            out((slots, size, size), BF),
            out((slots, size, size), F32),
            out((sectors, 1, size), F32),
        ),
    )


def correct_kernel(k, edges, slots, size, share, sectors, last):
    def body(meta, thetas, whole_image, whole_basis, shift, image, basis, state, *refs):
        meta = Meta(meta, edges, slots)
        bases = refs[: k - 1]
        if last:
            corrected, sums, new_state, stacked, sems = refs[2 * k - 2 :]
            sources = list(refs[k - 1 : 2 * k - 2]) + [image]
            copies = [
                pltpu.make_async_copy(source, stacked.at[j], sems.at[j])
                for j, source in enumerate(sources)
            ]
            for copy in copies:
                copy.start()
        else:
            whole, xin, corrected, sums, new_state = refs[k - 1 :]
        theta = jnp.sum(thetas[...].reshape(sectors, size), axis=0, keepdims=True)
        new_state[...] = state[...]
        new_state[k - 1 : k] = theta
        first_row = pl.multiple_of(meta.place() * share, share)

        def residual(mask, value, direction, moved):
            bottom = jnp.maximum(jnp.abs(moved - theta), 1.0)
            return jnp.where(mask, (value - theta * direction) / bottom, 0.0)

        def step(b, carry):
            direction = whole_basis[b]
            value = residual(
                mask_of(meta, b, (size, size), 0),
                whole_image[b].astype(F32),
                direction,
                shift[b],
            )
            if not last:
                whole[b] = value
                xin[b] = value.astype(BF)
            corrected[b] = residual(
                mask_of(meta, b, (share, size), first_row),
                image[b],
                basis[b],
                shift[b, pl.ds(first_row, share)],
            )
            others = [bases[j][b] for j in range(k - 1)] + [direction, value]
            return tuple(a + fold(value * o) for a, o in zip(carry, others))

        carry = lax.fori_loop(
            0, slots, step, tuple(jnp.zeros((8, size), F32) for _ in range(k + 1)), unroll=4
        )
        if last:
            line = lax.broadcasted_iota(jnp.int32, (EXTRA, size), 0)
            tail = jnp.zeros((EXTRA, size), F32)
            for j in range(k + 1):
                tail = jnp.where(line == j, total(carry[j]), tail)
            sums[...] = jnp.broadcast_to(tail[None], (sectors, EXTRA, size))
            for copy in copies:
                copy.wait()
        else:
            tail = jnp.zeros((EXTRA, size), F32)
            for j in range(k + 1):
                tail = tail + three_parts(total(carry[j]), j, EXTRA)
            sums[...] = tail

    blocks = out((slots, size, size), F32)
    shapes = [out((slots, share, size), F32), out((EXTRA, size), F32), out((24, size), F32)]
    if last:
        shapes[1] = out((sectors, EXTRA, size), F32)
        shapes.append(out((k, slots, share, size), F32))
        return call(
            body,
            "correct",
            [SMEM] + [VMEM] * (5 + 2 * k),
            tuple(shapes),
            [pltpu.SemaphoreType.DMA((k,))],
            out_specs=(VMEM, VMEM, VMEM, FAR),
        )
    shapes = [blocks, out((slots, size, size), BF)] + shapes
    return call(body, "correct", [SMEM] + [VMEM] * (6 + k), tuple(shapes))


def finish_kernel(slots, size, share, sectors):
    k = APPLIES

    def body(sums, vector, state, *refs):
        bases = refs[:k]
        final, ritz = refs[k:]
        added = jnp.sum(sums[...], axis=0)
        project = [added[j : j + 1] for j in range(k)]
        length = added[k : k + 1]
        for i in range(k):
            mixed = jnp.zeros((1, size), F32)
            for j in range(k):
                row = 8 + 4 * max(i, j) + min(i, j)
                mixed = mixed + state[row : row + 1] * project[j]
            length = length + project[i] * (mixed - 2.0 * project[i])
        scale = 1.0 / jnp.sqrt(jnp.maximum(length, 0.0) + 1e-6)
        for b in range(slots):
            value = vector[b]
            for j in range(k):
                value = value - project[j] * bases[j][b]
            final[b] = value * scale
        for j in range(k):
            ritz[j] = jnp.max(state[j : j + 1])

    return call(
        body,
        "finish",
        [VMEM] * (3 + k),
        (out((slots, share, size), F32), out((k,), F32)),
        out_specs=(VMEM, SMEM),
    )


def per_device(
    guess,
    diag_shift,
    block_rows,
    block_cols,
    left_env,
    right_env,
    edge_input,
    edge_left,
    edge_right,
    edge_owner,
    edge_slot,
):
    slots, size, _ = guess.shape
    sectors = lax.axis_size("sector")
    terms = lax.axis_size("mpo")
    edges = edge_input.shape[0]
    group = left_env.shape[0]
    share = size // terms
    chips = terms // 2
    place = lax.axis_index("mpo")
    core_swap = [(i, i ^ 1) for i in range(terms)]
    meta = jnp.concatenate(
        [
            edge_input,
            edge_left,
            edge_right,
            edge_owner[:, 0],
            edge_slot,
            block_rows,
            block_cols,
            place[None].astype(jnp.int32),
        ]
    )

    def over_sector(values):
        return lax.all_to_all(values, "sector", 0, 0, tiled=True)

    def chip_pair(values, k):
        pairs = [(i, 2 * ((i // 2) ^ k) + i % 2) for i in range(terms)]
        return lax.ppermute(values, "mpo", pairs)

    def chip_shift(values, k):
        pairs = [(i, (i + 2 * k) % terms) for i in range(terms)]
        return lax.ppermute(values, "mpo", pairs)

    def far(values):
        return pltpu.with_memory_space_constraint(values, pltpu.HBM)

    vector, xin, mine, sums, state, right_near, left_near = start_kernel(
        edges, slots, size, share, group
    )(meta, far(guess), far(right_env), far(left_env))
    bases, images, whole_bases, ids = [], [], [], []
    for k in range(1, APPLIES + 1):
        own, send, right_near, left_near = couple_kernel(edges, slots, size, share, group, chips)(
            meta, xin, right_near, left_near
        )
        received = lax.ppermute(send, "mpo", core_swap)
        parts = pair_kernel(edges, size, share, chips)(own, received)
        shifted = [parts[0]] + [chip_shift(parts[j], j) for j in range(1, chips)]
        message = pack_kernel(edges, slots, size, share, sectors, k == 1)(meta, sums, *shifted)
        arrived = over_sector(message)
        result = image_kernel(k, edges, slots, size, share, sectors)(
            meta, arrived, mine, state, *bases, *images, *ids
        )
        image, basis, outgoing, state = result[:4]
        if k == 1:
            ids = result[4:]
        rows = [outgoing] + [chip_pair(outgoing, j) for j in range(1, chips)]
        near_rows = gather_kernel(slots, size, share, chips)(*rows)
        far_rows = lax.ppermute(near_rows, "mpo", core_swap)
        whole_image, whole_basis, parts = weigh_kernel(
            k, edges, slots, size, share, sectors, chips
        )(
            meta, near_rows, far_rows, vector, state, *whole_bases
        )
        thetas = over_sector(parts)
        last = k == APPLIES
        others = [*whole_bases, *images] if last else whole_bases
        result = correct_kernel(k, edges, slots, size, share, sectors, last)(
            meta, thetas, whole_image, whole_basis, diag_shift, image, basis, state, *others
        )
        if last:
            mine, sums, state, stacked = result
        else:
            vector, xin, mine, sums, state = result
            whole_bases.append(whole_basis)
        bases.append(basis)
        images.append(image)
    final, ritz = finish_kernel(slots, size, share, sectors)(
        over_sector(sums), mine, state, *bases
    )
    return stacked, final, ritz


def solution(mesh):
    return jax.shard_map(
        per_device,
        mesh=mesh,
        in_specs=(
            P("sector", None, None),
            P("sector", None, None),
            P("sector"),
            P("sector"),
            P("mpo", "sector", None, None),
            P("mpo", "sector", None, None),
            P("sector"),
            P("sector"),
            P("sector"),
            P("sector", None),
            P("sector"),
        ),
        out_specs=(P(None, "sector", "mpo", None), P("sector", "mpo", None), P()),
        check_vma=False,
    )
```
